256 devices in a mesh: ctx: 32 (over z, x), head: 8 (over y, core).
Axes of the slice: x: 4, y: 4, z: 8, core: 2. Of those that a mesh axis runs over, the one named last changes fastest.
Arguments:
- queries: bfloat16 [8192, 8192], P('ctx', 'head'), may hold values from -20 to 20
- keys: bfloat16 [8192, 1024], P('ctx', 'head'), may hold values from -4 to 4
- values: bfloat16 [8192, 1024], P('ctx', 'head'), may hold values from -6 to 6
- grad_out: bfloat16 [8192, 8192], P('ctx', 'head'), may hold values from -6 to 6
- key_blocks: int32 [64, 6], replicated, may hold values from 0 to 63, as said below
- key_count: int32 [64], replicated, may hold values from 2 to 6
Outputs:
- attended: bfloat16 [8192, 8192], P('ctx', 'head')
- grad_q: bfloat16 [8192, 8192], P('ctx', 'head')
- grad_k: bfloat16 [8192, 1024], P('ctx', 'head')
- grad_v: bfloat16 [8192, 1024], P('ctx', 'head')
The draws below stay inside these ranges and needn't reach their ends.
Inputs may be any that keep to these rules, and one draw needn't show every extreme that they name: `key_blocks`: the listed key blocks of block b lie outside the range of 2 blocks that holds b (ranges begin at multiples of 2), each in a different range. Over the used slots of all query blocks of one range, at most 1 name blocks of any one other range; in every draw the query blocks of one range use all their 6 slots, so that this most and 12 used slots of one range are reached.
All inputs are finite; a program needn't handle non-finite values.
Results may differ from the reference program's by a relative error of at most 0.034.
Values may be sent and summed in bfloat16 or wider, within the bound.
A program may use at most 64 MiB of HBM per device.

```python
import math
import jax
import jax.numpy as jnp
from jax import lax

QH = 64
KVH = 8
DH = 128
BLOCK = 128
KSLOTS = 6
BLK_DEV = 2
SEQ = 8192
N_CTX = 32


def draw_queries(key, part):
    result = jnp.clip(jax.random.normal(jax.random.fold_in(key, 1), (SEQ, QH * DH), jnp.float32), -4.0, 4.0)
    return result.astype(jnp.bfloat16)


def draw_keys(key, part):
    result = jnp.clip(jax.random.normal(jax.random.fold_in(key, 2), (SEQ, KVH * DH), jnp.float32), -4.0, 4.0)
    return result.astype(jnp.bfloat16)


def block_lists(key):
    base_key = jax.random.fold_in(key, 11)
    subkeys = jax.random.split(base_key, 5)
    entries = BLK_DEV * KSLOTS
    orders = jax.vmap(lambda subkey: jax.random.permutation(subkey, N_CTX - 1))(jax.random.split(subkeys[0], N_CTX))
    device = jnp.arange(N_CTX)[:, None]
    owner_ids = (device + 1 + orders[:, jnp.arange(entries) % (N_CTX - 1)]) % N_CTX
    within = jax.random.randint(subkeys[1], (N_CTX, entries), 0, BLK_DEV)
    blocks = (owner_ids * BLK_DEV + within).reshape(N_CTX * BLK_DEV, KSLOTS)
    cap_rows = jax.random.randint(subkeys[2], (N_CTX, 1), 3, KSLOTS + 1)
    counts = jax.random.randint(subkeys[3], (N_CTX, BLK_DEV), cap_rows - 1, cap_rows + 1)
    heavy_ctx = jax.random.randint(subkeys[4], (), 0, N_CTX)
    counts = jnp.where(device == heavy_ctx, KSLOTS, counts)
    return (blocks.astype(jnp.int32), counts.reshape(N_CTX * BLK_DEV).astype(jnp.int32))


def draw_key_blocks(key, part):
    return block_lists(key)[0]


def draw_key_count(key, part):
    return block_lists(key)[1]


def steps_of(stream_key, extent, pieces, low, top_value):
    def one(axis_at, parts):
        heights = jax.random.uniform(jax.random.fold_in(jax.random.fold_in(stream_key, 6), axis_at), (parts,), jnp.float32, low / len(pieces), top_value / len(pieces))
        return jnp.repeat(jnp.exp(heights), extent[axis_at] // parts).reshape((-1,) + (1,) * (len(extent) - axis_at - 1))

    level = one(*pieces[0])
    for cut in pieces[1:]:
        level = level * one(*cut)
    return level


def normal_values(own_key, shape, scale, reach, cuts=(), held_as=jnp.bfloat16):
    values = jax.random.normal(own_key, shape, jnp.float32) * scale
    if len(cuts) > 0:
        values = steps_of(own_key, shape, cuts, -0.22, 0.18) * values
    return jnp.clip(values, min=-reach, max=reach).astype(held_as)


def setup_inputs(seed: int = 0) -> dict:
    arg_keys = jax.random.split(jax.random.key(seed), 7)
    queries = draw_queries(jax.random.fold_in(arg_keys[6], 71), 0)
    keys = draw_keys(jax.random.fold_in(arg_keys[6], 71), 0)
    values = normal_values(arg_keys[2], (SEQ, KVH * DH), 1.0, 6.0, ((0, 32), (1, 8)))
    grad_out = normal_values(arg_keys[3], (SEQ, QH * DH), 1.0, 6.0, ((0, 32), (1, 8)))
    key_blocks = draw_key_blocks(jax.random.fold_in(arg_keys[6], 71), 0)
    key_count = draw_key_count(jax.random.fold_in(arg_keys[6], 71), 0)
    return dict(queries=queries, keys=keys, values=values, grad_out=grad_out, key_blocks=key_blocks, key_count=key_count)


def reference(queries, keys, values, grad_out, key_blocks, key_count):
    group_size = QH // KVH
    scaling = 1.0 / math.sqrt(DH)
    block_count = SEQ // BLOCK
    key_width = (KSLOTS + 1) * BLOCK
    query_tiles = queries.reshape(block_count, BLOCK, KVH, group_size, DH)
    grad_tiles = grad_out.reshape(block_count, BLOCK, KVH, group_size, DH)
    key_tiles = keys.reshape(block_count, BLOCK, KVH, DH)
    value_tiles = values.reshape(block_count, BLOCK, KVH, DH)
    slot_ids = jnp.arange(KSLOTS, dtype=jnp.int32)

    def visit_block(carried, block_id):
        sum_k, sum_v = carried
        chosen = jnp.concatenate([block_id.reshape(1).astype(jnp.int32), key_blocks[block_id].astype(jnp.int32)])
        is_live = jnp.concatenate([jnp.ones((1,), dtype=bool), slot_ids < key_count[block_id]])
        column = jnp.repeat(is_live, BLOCK)
        near_k = key_tiles[chosen].reshape(key_width, KVH, DH).astype(jnp.float32)
        near_v = value_tiles[chosen].reshape(key_width, KVH, DH).astype(jnp.float32)
        query_tile = query_tiles[block_id].astype(jnp.float32)
        grad_tile = grad_tiles[block_id].astype(jnp.float32)
        scores = jnp.einsum('qhgd,khd->hgqk', query_tile, near_k) * scaling
        scores = jnp.where(column, scores, -1e+30)
        row_max = lax.optimization_barrier(jnp.max(scores, axis=-1, keepdims=True))
        expo_terms = jnp.where(column, jnp.exp(scores - row_max), 0.0)
        prob_rows = expo_terms / lax.optimization_barrier(jnp.sum(expo_terms, axis=-1, keepdims=True))
        weights = lax.optimization_barrier(prob_rows.astype(jnp.bfloat16)).astype(jnp.float32)
        attended = jnp.einsum('hgqk,khd->qhgd', weights, near_v).astype(jnp.bfloat16)
        delta_rows = lax.optimization_barrier(jnp.sum(grad_tile * attended.astype(jnp.float32), axis=-1))
        grad_p = jnp.einsum('qhgd,khd->hgqk', grad_tile, near_v)
        grad_s = prob_rows * (grad_p - jnp.transpose(delta_rows, (1, 2, 0))[..., None]) * scaling
        grad_s = lax.optimization_barrier(grad_s.astype(jnp.bfloat16)).astype(jnp.float32)
        grad_q = jnp.einsum('hgqk,khd->qhgd', grad_s, near_k).astype(jnp.bfloat16)
        part_k = jnp.einsum('hgqk,qhgd->khd', grad_s, query_tile).reshape(KSLOTS + 1, BLOCK, KVH, DH)
        part_v = jnp.einsum('hgqk,qhgd->khd', weights, grad_tile).reshape(KSLOTS + 1, BLOCK, KVH, DH)
        sum_k = sum_k.at[chosen].add(part_k)
        sum_v = sum_v.at[chosen].add(part_v)
        return ((sum_k, sum_v), (attended, grad_q))
    start_sums = (jnp.zeros((block_count, BLOCK, KVH, DH), jnp.float32), jnp.zeros((block_count, BLOCK, KVH, DH), jnp.float32))
    (sum_k, sum_v), (attended, grad_q) = lax.scan(visit_block, start_sums, jnp.arange(block_count, dtype=jnp.int32))
    return (attended.reshape(SEQ, QH * DH), grad_q.reshape(SEQ, QH * DH), sum_k.astype(jnp.bfloat16).reshape(SEQ, KVH * DH), sum_v.astype(jnp.bfloat16).reshape(SEQ, KVH * DH))
```

```python
import functools, math
import jax, jax.numpy as jnp
from jax import lax
from jax.experimental import pallas as pl
from jax.experimental.pallas import tpu as pltpu
from jax.sharding import PartitionSpec as P

QH = 64
KVH = 8
DH = 128
BLOCK = 128
KSLOTS = 6
NSLOT = KSLOTS + 1
GROUP = QH // KVH
SCALING = 1.0 / math.sqrt(DH)
LOG2E = 1.4426950408889634
NEG = -1e30


def attn_kernel(kb, kc, pos, q_ref, o_ref, own_ref, *rest):
    far = rest[:KSLOTS]
    att_ref, gq_ref, gown_ref, contrib_ref = rest[KSLOTS:KSLOTS + 4]
    k_s, v_s, kt_s, vt_s, s_s, dp_s, p_s, ds_s, dk_s, dv_s = rest[KSLOTS + 4:]
    b = pl.program_id(0)
    blk = pos[0] * pl.num_programs(0) + b
    count = kc[blk]

    @pl.when(b == 0)
    def _():
        contrib_ref[...] = jnp.zeros_like(contrib_ref)

    for s in range(NSLOT):
        src = own_ref if s == 0 else far[s - 1]
        rows = slice(s * BLOCK, (s + 1) * BLOCK)
        k = src[:, :DH]
        v = src[:, DH:]
        k_s[rows, :] = k
        v_s[rows, :] = v
        kt_s[:, rows] = k.T
        vt_s[:, rows] = v.T
    bias = [None] + [jnp.where(s < count, 0.0, NEG).astype(jnp.float32) for s in range(KSLOTS)]
    c = SCALING * LOG2E
    nt = (((1,), (1,)), ((), ()))

    for pair in range(GROUP // 2):
        cols = [slice((2 * pair + i) * DH, (2 * pair + i + 1) * DH) for i in range(2)]
        q2 = jnp.concatenate([q_ref[:, cols[0]], q_ref[:, cols[1]]], axis=0)
        o2 = jnp.concatenate([o_ref[:, cols[0]], o_ref[:, cols[1]]], axis=0)
        m = None
        for s in range(NSLOT):
            rows = slice(s * BLOCK, (s + 1) * BLOCK)
            sc = lax.dot_general(k_s[rows, :], q2, nt, preferred_element_type=jnp.float32)
            s_s[rows, :] = sc
            top = jnp.max(sc, axis=0, keepdims=True)
            if s > 0:
                top = top + bias[s]
            m = top if m is None else jnp.maximum(m, top)
        mc = m * c
        total = None
        for s in range(NSLOT):
            rows = slice(s * BLOCK, (s + 1) * BLOCK)
            off = -mc if s == 0 else bias[s] - mc
            e = jnp.exp2(s_s[rows, :] * c + off)
            s_s[rows, :] = e
            part = jnp.sum(e, axis=0, keepdims=True)
            total = part if total is None else total + part
        inv = 1.0 / total
        for s in range(NSLOT):
            rows = slice(s * BLOCK, (s + 1) * BLOCK)
            p_s[rows, :] = (s_s[rows, :] * inv).astype(jnp.bfloat16)
        p16 = p_s[...]
        out_t = jnp.dot(vt_s[...], p16, preferred_element_type=jnp.float32)
        att_t = out_t.astype(jnp.bfloat16)
        o_t = o2.T.astype(jnp.float32)
        delta = jnp.sum(o_t * att_t.astype(jnp.float32), axis=0, keepdims=True)
        att = att_t.T
        att_ref[:, cols[0]] = att[:BLOCK]
        att_ref[:, cols[1]] = att[BLOCK:]
        dv = jnp.dot(p16, o2, preferred_element_type=jnp.float32)
        if pair == 0:
            dv_s[...] = dv
        else:
            dv_s[...] += dv
        inv_c = inv * SCALING
        for s in range(NSLOT):
            rows = slice(s * BLOCK, (s + 1) * BLOCK)
            dp = lax.dot_general(v_s[rows, :], o2, nt, preferred_element_type=jnp.float32)
            ds_s[rows, :] = ((s_s[rows, :] * inv_c) * (dp - delta)).astype(jnp.bfloat16)
        ds16 = ds_s[...]
        gq = jnp.dot(kt_s[...], ds16, preferred_element_type=jnp.float32).astype(jnp.bfloat16).T
        gq_ref[:, cols[0]] = gq[:BLOCK]
        gq_ref[:, cols[1]] = gq[BLOCK:]
        dk = jnp.dot(ds16, q2, preferred_element_type=jnp.float32)
        if pair == 0:
            dk_s[...] = dk
        else:
            dk_s[...] += dk
    gown_ref[:, :DH] = dk_s[:BLOCK, :]
    gown_ref[:, DH:] = dv_s[:BLOCK, :]
    for s in range(KSLOTS):
        rows = slice((s + 1) * BLOCK, (s + 2) * BLOCK)

        @pl.when(s < count)
        def _():
            at = kb[blk * KSLOTS + s]
            contrib_ref[at, :, :DH] = dk_s[rows, :].astype(jnp.bfloat16)
            contrib_ref[at, :, DH:] = dv_s[rows, :].astype(jnp.bfloat16)


def attention(kb, kc, pos, q, o, own, every):
    rows, width = q.shape
    blocks = rows // BLOCK
    n_all = every.shape[0]
    row = lambda b, kb, kc, pos: (b, 0)
    def far(s):
        return pl.BlockSpec((pl.Squeezed(), BLOCK, 2 * DH), lambda b, kb, kc, pos: (kb[(pos[0] * blocks + b) * KSLOTS + s], 0, 0))
    wide = NSLOT * BLOCK
    spec = pltpu.PrefetchScalarGridSpec(
        num_scalar_prefetch=3,
        grid=(blocks,),
        in_specs=[pl.BlockSpec((BLOCK, width), row), pl.BlockSpec((BLOCK, width), row), pl.BlockSpec((BLOCK, 2 * DH), row)] + [far(s) for s in range(KSLOTS)],
        out_specs=[pl.BlockSpec((BLOCK, width), row), pl.BlockSpec((BLOCK, width), row), pl.BlockSpec((BLOCK, 2 * DH), row), pl.BlockSpec((n_all, BLOCK, 2 * DH), lambda b, kb, kc, pos: (0, 0, 0))],
        scratch_shapes=[pltpu.VMEM((wide, DH), jnp.bfloat16)] * 2 + [pltpu.VMEM((DH, wide), jnp.bfloat16)] * 2
        + [pltpu.VMEM((wide, 2 * BLOCK), jnp.float32)] * 2 + [pltpu.VMEM((wide, 2 * BLOCK), jnp.bfloat16)] * 2 + [pltpu.VMEM((wide, DH), jnp.float32)] * 2,
    )
    return pl.pallas_call(
        attn_kernel,
        grid_spec=spec,
        out_shape=[jax.ShapeDtypeStruct((rows, width), jnp.bfloat16)] * 2 + [jax.ShapeDtypeStruct((rows, 2 * DH), jnp.float32), jax.ShapeDtypeStruct((n_all, BLOCK, 2 * DH), jnp.bfloat16)],
        compiler_params=pltpu.CompilerParams(vmem_limit_bytes=48 << 20),
        name="attention",
    )(kb, kc, pos, q, o, own, *([every] * KSLOTS))


def local(queries, keys, values, grad_out, key_blocks, key_count):
    rows = queries.shape[0]
    pos = lax.axis_index("ctx").astype(jnp.int32).reshape(1)
    own = jnp.concatenate([keys, values], axis=1)
    every = lax.all_gather(own, "ctx", axis=0, tiled=True).reshape(-1, BLOCK, 2 * DH)
    att, gq, gown, contrib = attention(key_blocks.reshape(-1), key_count, pos, queries, grad_out, own, every)
    mine = lax.psum_scatter(contrib, "ctx", scatter_dimension=0, tiled=True)
    total = (gown + mine.reshape(rows, 2 * DH).astype(jnp.float32)).astype(jnp.bfloat16)
    return att, gq, total[:, :DH], total[:, DH:]


def solution(mesh):
    in_specs = (P("ctx", "head"), P("ctx", "head"), P("ctx", "head"), P("ctx", "head"), P(), P())
    out_specs = (P("ctx", "head"), P("ctx", "head"), P("ctx", "head"), P("ctx", "head"))
    return jax.shard_map(local, mesh=mesh, in_specs=in_specs, out_specs=out_specs, check_vma=False)
```

```python
import functools, math
import jax, jax.numpy as jnp
from jax import lax
from jax.experimental import pallas as pl
from jax.experimental.pallas import tpu as pltpu
from jax.sharding import PartitionSpec as P

QH = 64
KVH = 8
DH = 128
BLOCK = 128
KSLOTS = 6
NSLOT = KSLOTS + 1
GROUP = QH // KVH
SCALING = 1.0 / math.sqrt(DH)
LOG2E = 1.4426950408889634
NEG = -1e30


def attn_kernel(kb, kc, pos, q_ref, o_ref, k_own, v_own, *rest):
    far_k, far_v = rest[:KSLOTS], rest[KSLOTS:2 * KSLOTS]
    att_ref, gq_ref, gk_ref, gv_ref, ck_ref, cv_ref = rest[2 * KSLOTS:2 * KSLOTS + 6]
    k_s, v_s, kt_s, vt_s, s_s, p_s, ds_s, dk_s, dv_s = rest[2 * KSLOTS + 6:]
    b = pl.program_id(0)
    blk = pos[0] * pl.num_programs(0) + b
    count = kc[blk]

    @pl.when(b == 0)
    def _():
        ck_ref[...] = jnp.zeros_like(ck_ref)
        cv_ref[...] = jnp.zeros_like(cv_ref)

    for s in range(NSLOT):
        rows = slice(s * BLOCK, (s + 1) * BLOCK)
        k = (k_own if s == 0 else far_k[s - 1])[...]
        v = (v_own if s == 0 else far_v[s - 1])[...]
        k_s[rows, :] = k
        v_s[rows, :] = v
        kt_s[:, rows] = k.T
        vt_s[:, rows] = v.T
    bias = [None] + [jnp.where(s < count, 0.0, NEG).astype(jnp.float32) for s in range(KSLOTS)]
    c = SCALING * LOG2E
    nt = (((1,), (1,)), ((), ()))

    for pair in range(GROUP // 2):
        cols = [slice((2 * pair + i) * DH, (2 * pair + i + 1) * DH) for i in range(2)]
        q2 = jnp.concatenate([q_ref[:, cols[0]], q_ref[:, cols[1]]], axis=0)
        o2 = jnp.concatenate([o_ref[:, cols[0]], o_ref[:, cols[1]]], axis=0)
        m = None
        for s in range(NSLOT):
            rows = slice(s * BLOCK, (s + 1) * BLOCK)
            sc = lax.dot_general(k_s[rows, :], q2, nt, preferred_element_type=jnp.float32)
            s_s[rows, :] = sc
            top = jnp.max(sc, axis=0, keepdims=True)
            if s > 0:
                top = top + bias[s]
            m = top if m is None else jnp.maximum(m, top)
        mc = m * c
        total = None
        for s in range(NSLOT):
            rows = slice(s * BLOCK, (s + 1) * BLOCK)
            off = -mc if s == 0 else bias[s] - mc
            e = jnp.exp2(s_s[rows, :] * c + off)
            s_s[rows, :] = e
            part = jnp.sum(e, axis=0, keepdims=True)
            total = part if total is None else total + part
        inv = 1.0 / total
        for s in range(NSLOT):
            rows = slice(s * BLOCK, (s + 1) * BLOCK)
            p_s[rows, :] = (s_s[rows, :] * inv).astype(jnp.bfloat16)
        p16 = p_s[...]
        out_t = jnp.dot(vt_s[...], p16, preferred_element_type=jnp.float32)
        att_t = out_t.astype(jnp.bfloat16)
        o_t = o2.T.astype(jnp.float32)
        delta = jnp.sum(o_t * att_t.astype(jnp.float32), axis=0, keepdims=True)
        att = att_t.T
        att_ref[:, cols[0]] = att[:BLOCK]
        att_ref[:, cols[1]] = att[BLOCK:]
        dv = jnp.dot(p16, o2, preferred_element_type=jnp.float32)
        if pair == 0:
            dv_s[...] = dv
        else:
            dv_s[...] += dv
        inv_c = inv * SCALING
        for s in range(NSLOT):
            rows = slice(s * BLOCK, (s + 1) * BLOCK)
            dp = lax.dot_general(v_s[rows, :], o2, nt, preferred_element_type=jnp.float32)
            ds_s[rows, :] = ((s_s[rows, :] * inv_c) * (dp - delta)).astype(jnp.bfloat16)
        ds16 = ds_s[...]
        gq = jnp.dot(kt_s[...], ds16, preferred_element_type=jnp.float32).astype(jnp.bfloat16).T
        gq_ref[:, cols[0]] = gq[:BLOCK]
        gq_ref[:, cols[1]] = gq[BLOCK:]
        dk = jnp.dot(ds16, q2, preferred_element_type=jnp.float32)
        if pair == 0:
            dk_s[...] = dk
        else:
            dk_s[...] += dk
    gk_ref[...] = dk_s[:BLOCK, :]
    gv_ref[...] = dv_s[:BLOCK, :]
    for s in range(KSLOTS):
        rows = slice((s + 1) * BLOCK, (s + 2) * BLOCK)

        @pl.when(s < count)
        def _():
            at = kb[blk * KSLOTS + s]
            ck_ref[at] = dk_s[rows, :].astype(jnp.bfloat16)
            cv_ref[at] = dv_s[rows, :].astype(jnp.bfloat16)


def attention(kb, kc, pos, q, o, k_own, v_own, k_all, v_all):
    rows, width = q.shape
    blocks = rows // BLOCK
    n_all = k_all.shape[0]
    row = lambda b, kb, kc, pos: (b, 0)

    def far(s):
        def index(b, kb, kc, pos):
            blk = pos[0] * blocks + b
            return (kb[blk * KSLOTS + jnp.where(s < kc[blk], s, 0)], 0, 0)

        return pl.BlockSpec((pl.Squeezed(), BLOCK, DH), index)

    wide_spec = pl.BlockSpec((BLOCK, width), row)
    own_spec = pl.BlockSpec((BLOCK, DH), row)
    all_spec = pl.BlockSpec((n_all, BLOCK, DH), lambda b, kb, kc, pos: (0, 0, 0))
    wide = NSLOT * BLOCK
    spec = pltpu.PrefetchScalarGridSpec(
        num_scalar_prefetch=3,
        grid=(blocks,),
        in_specs=[wide_spec] * 2 + [own_spec] * 2 + [far(s) for s in range(KSLOTS)] * 2,
        out_specs=[wide_spec] * 2 + [own_spec] * 2 + [all_spec] * 2,
        scratch_shapes=[pltpu.VMEM((wide, DH), jnp.bfloat16)] * 2 + [pltpu.VMEM((DH, wide), jnp.bfloat16)] * 2
        + [pltpu.VMEM((wide, 2 * BLOCK), jnp.float32)] + [pltpu.VMEM((wide, 2 * BLOCK), jnp.bfloat16)] * 2 + [pltpu.VMEM((wide, DH), jnp.float32)] * 2,
    )
    out = lambda shape, dtype: jax.ShapeDtypeStruct(shape, dtype)
    return pl.pallas_call(
        attn_kernel,
        grid_spec=spec,
        out_shape=[out((rows, width), jnp.bfloat16)] * 2 + [out((rows, DH), jnp.float32)] * 2 + [out((n_all, BLOCK, DH), jnp.bfloat16)] * 2,
        compiler_params=pltpu.CompilerParams(vmem_limit_bytes=48 << 20),
        name="attention",
    )(kb, kc, pos, q, o, k_own, v_own, *([k_all] * KSLOTS), *([v_all] * KSLOTS))


XN = 4
MESH = pl.DeviceIdType.MESH


class Tree:
    def __init__(self, first, n):
        position = lax.axis_index("ctx")
        sizes = {"x": XN, "z": n // XN}
        coords = {"x": lax.rem(position, XN), "z": lax.div(position, XN)}
        self.first = first
        self.na, self.nb = sizes[first], sizes["z" if first == "x" else "x"]
        self.a, self.b = coords[first], coords["z" if first == "x" else "x"]

    def at(self, da, db):
        a = lax.rem(self.a + (da % self.na), self.na)
        b = lax.rem(self.b + (db % self.nb), self.nb)
        return b * XN + a if self.first == "x" else a * XN + b

    def keys(self):
        out = [(1, 0, d, t) for t in range(1, self.na // 2 + 1) for d in (1, -1)]
        for da in range(self.na):
            out += [(2, da, d, t) for t in range(1, self.nb // 2 + 1) for d in (1, -1)]
        return out

    def length(self, stage):
        return self.na if stage == 1 else self.nb

    def step(self, stage, d):
        return self.at(d, 0) if stage == 1 else self.at(0, d)

    def span(self, stage, d, t, rows):
        if t * 2 < self.length(stage):
            return pl.ds(0, rows)
        return pl.ds(0 if d == 1 else rows // 2, rows // 2)


def far_first(n):
    return sorted(range(n), key=lambda o: (-min(o, n - o), o))


def meet(n):
    barrier = pltpu.get_barrier_semaphore()
    tree = Tree("x", n)
    for stage in (1, 2):
        for d in (1, -1):
            pl.semaphore_signal(barrier, inc=1, device_id={"ctx": tree.step(stage, d)}, device_id_type=MESH)
    pl.semaphore_wait(barrier, 4)


def gather_kernel(n, k_ref, v_ref, k_all, v_all, send_sem, recv_sem):
    rows = k_ref.shape[0]
    trees = [Tree("x", n), Tree("z", n)]
    own = [k_ref, v_ref]
    every = [k_all, v_all]
    number = {}
    for i, tree in enumerate(trees):
        for key in tree.keys():
            number[(i,) + key] = len(number)
    meet(n)
    sent = []

    def send(i, stage, da, d, t, src, slot):
        tree = trees[i]
        span = tree.span(stage, d, t, rows)
        at = number[(i, stage, da, d, t)]
        copy = pltpu.make_async_remote_copy(
            src_ref=src.at[span], dst_ref=every[i].at[slot, span],
            send_sem=send_sem.at[at], recv_sem=recv_sem.at[at],
            device_id={"ctx": tree.step(stage, d)}, device_id_type=MESH)
        copy.start()
        sent.append(copy)

    def origin(i, stage, da, d, t):
        tree = trees[i]
        return tree.at(-d * t, 0) if stage == 1 else tree.at(da, -d * t)

    def await_one(i, stage, da, d, t):
        tree = trees[i]
        slot = origin(i, stage, da, d, t)
        span = tree.span(stage, d, t, rows)
        at = number[(i, stage, da, d, t)]
        pltpu.make_async_remote_copy(
            src_ref=every[i].at[slot, span], dst_ref=every[i].at[slot, span],
            send_sem=send_sem.at[at], recv_sem=recv_sem.at[at],
            device_id={"ctx": tree.step(stage, -d)}, device_id_type=MESH).wait_recv()
        if t * 2 < tree.length(stage):
            send(i, stage, da, d, t + 1, every[i].at[slot], slot)

    def spread(i, da):
        slot = trees[i].at(da, 0)
        src = own[i] if da == 0 else every[i].at[slot]
        for d in (1, -1):
            send(i, 2, da, d, 1, src, slot)

    for i in (1, 0):
        for d in (1, -1):
            send(i, 1, 0, d, 1, own[i], trees[i].at(0, 0))
    for i in (0, 1):
        spread(i, 0)

    events = []
    for i, tree in enumerate(trees):
        pace = 1.2
        for t in range(1, tree.na // 2 + 1):
            events.append((1.0 + 1.3 * (t - 1), i, 1, 0, t))
        near = [o for o in reversed(far_first(tree.na))]
        for j, da in enumerate(near):
            for t in range(1, tree.nb // 2 + 1):
                events.append((1.5 + pace * j + pace * tree.na * (t - 1), i, 2, da, t))
    for _, i, stage, da, t in sorted(events):
        tree = trees[i]
        for d in (1, -1):
            await_one(i, stage, da, d, t)
            if stage == 1 and t * 2 < tree.na:
                spread(i, (-d * t) % tree.na)
        if stage == 1 and t * 2 == tree.na:
            spread(i, t)
    for copy in sent:
        copy.wait_send()


def gather(n, k, v, copies):
    shape = jax.ShapeDtypeStruct((n,) + k.shape, k.dtype)
    return pl.pallas_call(
        functools.partial(gather_kernel, n),
        out_shape=[shape, shape],
        in_specs=[pl.BlockSpec(memory_space=pl.ANY)] * 2,
        out_specs=[pl.BlockSpec(memory_space=pl.ANY)] * 2,
        scratch_shapes=[pltpu.SemaphoreType.DMA((copies,))] * 2,
        compiler_params=pltpu.CompilerParams(collective_id=0, has_side_effects=True),
        name="gather",
    )(k, v)


def scatter_kernel(n, ck_ref, cv_ref, gk_ref, gv_ref, outk_ref, outv_ref, land, sums_k, sums_v, send_sem, recv_sem):
    rows = gk_ref.shape[0]
    trees = [Tree("x", n), Tree("z", n)]
    terms = [ck_ref, cv_ref]
    sums = [sums_k, sums_v]
    number = {}
    for i, tree in enumerate(trees):
        for key in tree.keys():
            number[(i,) + key] = len(number)
    meet(n)
    sent = []

    def send(i, stage, da, d, t, src):
        tree = trees[i]
        span = tree.span(stage, d, t, rows)
        at = number[(i, stage, da, d, t)]
        copy = pltpu.make_async_remote_copy(
            src_ref=src.at[span], dst_ref=land.at[at, span],
            send_sem=send_sem.at[at], recv_sem=recv_sem.at[at],
            device_id={"ctx": tree.step(stage, -d)}, device_id_type=MESH)
        copy.start()
        sent.append(copy)

    def arrive(i, stage, da, d, t):
        tree = trees[i]
        span = tree.span(stage, d, t, rows)
        at = number[(i, stage, da, d, t)]
        pltpu.make_async_remote_copy(
            src_ref=land.at[at, span], dst_ref=land.at[at, span],
            send_sem=send_sem.at[at], recv_sem=recv_sem.at[at],
            device_id={"ctx": tree.step(stage, d)}, device_id_type=MESH).wait_recv()
        return at, span

    def pass_on(i, stage, da, d, t, load):
        tree = trees[i]
        at, span = arrive(i, stage, da, d, t + 1)
        half = rows // 2
        whole = (t + 1) * 2 < tree.length(stage)
        for part in (0, 1):
            here = pl.ds(part * half, half)
            mine = load(here)
            if whole or part == (0 if d == 1 else 1):
                mine = (mine.astype(jnp.float32) + land[at, here].astype(jnp.float32)).astype(jnp.bfloat16)
            land[at, here] = mine
        send(i, stage, da, d, t, land.at[at])

    def close(i, da):
        tree = trees[i]
        first, _ = arrive(i, 2, da, 1, 1)
        second, _ = arrive(i, 2, da, -1, 1)
        total = land[first].astype(jnp.float32) + land[second].astype(jnp.float32)
        if da != 0:
            total = total + terms[i][tree.at(da, 0)].astype(jnp.float32)
            sums[i][da] = total.astype(jnp.bfloat16)
            if da * 2 == tree.na:
                for d in (1, -1):
                    send(i, 1, 0, d, da, sums[i].at[da])
            return
        out = (outk_ref, outv_ref)[i]
        grown = (gk_ref, gv_ref)[i]
        for d in (1, -1):
            at, _ = arrive(i, 1, 0, d, 1)
            total = total + land[at].astype(jnp.float32)
        out[...] = (total + grown[...]).astype(jnp.bfloat16)

    def start(i, da):
        tree = trees[i]
        for d in (1, -1):
            t = tree.nb // 2
            send(i, 2, da, d, t, terms[i].at[tree.at(da, t)])

    orders = [far_first(tree.na) for tree in trees]
    for j in range(max(tree.na for tree in trees)):
        for i in (0, 1):
            if j < trees[i].na:
                start(i, orders[i][j])
    events = []
    for i, tree in enumerate(trees):
        top = tree.nb // 2
        half = tree.na * 0.5
        for j, da in enumerate(orders[i]):
            for t in range(top - 1, 0, -1):
                arrival = 0.5 * (j + 1) if t + 1 == top else half + tree.na * (top - t - 2) + j + 1
                events.append((arrival, i, 2, da, t))
            events.append((half + tree.na * (top - 2) + j + 1, i, 2, da, 0))
        for t in range(tree.na // 2 - 1, 0, -1):
            ready = half + tree.na * (top - 2) + 2 * (tree.na // 2 - t) + 2
            events.append((ready, i, 1, 0, t))
    events.sort()
    for _, i, stage, da, t in events:
        tree = trees[i]
        if stage == 2 and t > 0:
            for d in (1, -1):
                target = tree.at(da, -d * t)
                pass_on(i, 2, da, d, t, lambda here, i=i, target=target: terms[i][target, here])
        elif stage == 2:
            if da != 0:
                close(i, da)
        else:
            for d in (1, -1):
                pass_on(i, 1, 0, d, t, lambda here, i=i, o=(-d * t) % tree.na: sums[i][o, here])
    for i in (0, 1):
        close(i, 0)
    for copy in sent:
        copy.wait_send()


def scatter(n, ck, cv, gk, gv, copies):
    rows, width = gk.shape
    vmem = pl.BlockSpec(memory_space=pltpu.VMEM)
    shape = jax.ShapeDtypeStruct((rows, width), jnp.bfloat16)
    return pl.pallas_call(
        functools.partial(scatter_kernel, n),
        out_shape=[shape, shape],
        in_specs=[vmem] * 4,
        out_specs=[vmem] * 2,
        scratch_shapes=[pltpu.VMEM((copies, rows, width), jnp.bfloat16),
                        pltpu.VMEM((XN, rows, width), jnp.bfloat16),
                        pltpu.VMEM((n // XN, rows, width), jnp.bfloat16),
                        pltpu.SemaphoreType.DMA((copies,)), pltpu.SemaphoreType.DMA((copies,))],
        compiler_params=pltpu.CompilerParams(collective_id=1, has_side_effects=True, vmem_limit_bytes=48 << 20),
        name="scatter",
    )(ck, cv, gk, gv)


def copies_of(n):
    total = 0
    for na, nb in ((XN, n // XN), (n // XN, XN)):
        total += 2 * (na // 2) + na * 2 * (nb // 2)
    return total


def local(queries, keys, values, grad_out, key_blocks, key_count):
    n = lax.axis_size("ctx")
    rows = keys.shape[0]
    pos = lax.axis_index("ctx").astype(jnp.int32).reshape(1)
    copies = copies_of(n)
    k_all, v_all = gather(n, keys, values, copies)
    k_all, v_all = (a.reshape(-1, BLOCK, DH) for a in (k_all, v_all))
    att, gq, gk, gv, ck, cv = attention(
        key_blocks.reshape(-1), key_count, pos, queries, grad_out, keys, values, k_all, v_all)
    grad_k, grad_v = scatter(n, ck.reshape(n, rows, DH), cv.reshape(n, rows, DH), gk, gv, copies)
    return att, gq, grad_k, grad_v


def solution(mesh):
    in_specs = (P("ctx", "head"), P("ctx", "head"), P("ctx", "head"), P("ctx", "head"), P(), P())
    out_specs = (P("ctx", "head"), P("ctx", "head"), P("ctx", "head"), P("ctx", "head"))
    return jax.shard_map(local, mesh=mesh, in_specs=in_specs, out_specs=out_specs, check_vma=False)
```

```python
import functools
import math

import jax
import jax.numpy as jnp
from jax import lax
from jax.experimental import pallas as pl
from jax.experimental.pallas import tpu as pltpu
from jax.sharding import PartitionSpec as P

QH = 64
KVH = 8
DH = 128
BLOCK = 128
KSLOTS = 6
NSLOT = KSLOTS + 1
GROUP = QH // KVH
BLK_DEV = 2
ENTRIES = BLK_DEV * KSLOTS
XN = 4
ZN = 8
HALF = BLOCK // 2
FAR = (XN - 1) * ZN
WIDE = NSLOT * BLOCK
SCALING = 1.0 / math.sqrt(DH)
SCALE2 = SCALING * 1.4426950408889634
NEG = -1e30
COPIES = 160
MESH = pl.DeviceIdType.MESH
BF16 = jnp.bfloat16
F32 = jnp.float32
NT = (((1,), (1,)), ((), ()))


def place(u):
    return 0 if u == 0 else (2 * u - 1 if u <= ZN // 2 else 2 * (ZN - u))


GROUPS = [(0, 1)] + [(2 * t - 1, 2) for t in range(1, ZN // 2)] + [(ZN - 1, 1)]
RANGE_AT = sorted(range(ZN), key=place)


def kernel(kb, kc, q_hbm, o_hbm, k_hbm, v_hbm, att_hbm, gq_hbm, outk_ref, outv_ref,
           q_in, o_in, att_s, gq_s, near_k, near_v, stage, transit, terms, ring, rowsum,
           parts_k, parts_v, own_k, own_v, k_s, v_s, kt_s, vt_s, q_st, o_st, e_s, p_s, ds_s, inv_s,
           which_s, slot_s, load_s, send_sem, recv_sem, local_sem):
    position = lax.axis_index("ctx")
    x = lax.rem(position, XN)
    z = lax.div(position, XN)
    near = [near_k, near_v]
    kv_hbm = [k_hbm, v_hbm]

    def along_x(dx):
        return z * XN + lax.rem(x + dx % XN, XN)

    def along_z(dz):
        return lax.rem(z + dz % ZN, ZN) * XN + x

    barrier = pltpu.get_barrier_semaphore()
    for d in (1, -1):
        pl.semaphore_signal(barrier, inc=1, device_id={"ctx": along_x(d)}, device_id_type=MESH)
        pl.semaphore_signal(barrier, inc=1, device_id={"ctx": along_z(d)}, device_id_type=MESH)

    loads = []
    for i, (src, dst) in enumerate((
            (k_hbm, near_k.at[pl.ds(FAR, BLK_DEV)]), (v_hbm, near_v.at[pl.ds(FAR, BLK_DEV)]),
            (q_hbm, q_in), (o_hbm, o_in))):
        copy = pltpu.make_async_copy(src, dst, local_sem.at[i])
        copy.start()
        loads.append(copy)

    for dx in range(XN):
        reader = along_x(dx) * BLK_DEV
        blocks, owners = [], []
        for e in range(ENTRIES):
            block = kb[reader + e // KSLOTS, e % KSLOTS]
            live = e % KSLOTS < kc[reader + e // KSLOTS]
            blocks.append(lax.rem(block, BLK_DEV))
            owners.append(jnp.where(live, lax.div(block, BLK_DEV), -1))
        for u in range(ZN):
            wanted = along_z(u)
            which = jnp.int32(0)
            for e in range(ENTRIES):
                which = jnp.where(owners[e] == wanted, blocks[e], which)
            which_s[dx * ZN + u] = which
        if dx == 0:
            for ax in range(XN):
                for u in range(ZN):
                    wanted = lax.rem(z + u, ZN) * XN + lax.rem(x + ax, XN)
                    slot = jnp.int32(ENTRIES)
                    for e in range(ENTRIES):
                        slot = jnp.where(owners[e] == wanted, e, slot)
                    slot_s[ax * ZN + u] = slot
    for b in range(BLK_DEV):
        block = position * BLK_DEV + b
        first = None
        for s in range(KSLOTS):
            listed = kb[block, s]
            owner = lax.div(listed, BLK_DEV)
            dx = lax.rem(lax.rem(owner, XN) - x + XN, XN)
            u = lax.rem(lax.div(owner, XN) - z + ZN, ZN)
            spot = jnp.where(u == 0, 0, jnp.where(u <= ZN // 2, 2 * u - 1, 2 * (ZN - u)))
            at = jnp.where(dx == 0, FAR + BLK_DEV * u + lax.rem(listed, BLK_DEV), (dx - 1) * ZN + spot)
            first = at if s == 0 else first
            load_s[b * KSLOTS + s] = jnp.where(s < kc[block], at, first)

    used = [0]
    sent = []

    def send(src, dst, device):
        at = used[0]
        used[0] += 1
        copy = pltpu.make_async_remote_copy(
            src_ref=src, dst_ref=dst, send_sem=send_sem.at[at], recv_sem=recv_sem.at[at],
            device_id={"ctx": device}, device_id_type=MESH)
        copy.start()
        sent.append(copy)
        return copy

    def column(i, u, t, d):
        first = FAR + BLK_DEV * (u % ZN)
        if 2 * t < ZN:
            return near[i].at[pl.ds(first, BLK_DEV)]
        return near[i].at[pl.ds(first + (0 if d == 1 else 1), 1)]

    def ring_send(i, t):
        out = []
        for d in (1, -1):
            u = -d * (t - 1)
            if t > 1:
                src = column(i, u, t, d)
            else:
                src = kv_hbm[i]
            out.append(send(src, column(i, u - d, t, d), along_z(d)))
        return out

    def spread(phase, group, dst):
        first, count = group
        here = pl.ds(first, count)
        out = []
        for d in (1, -1):
            a = (d - 1) % XN
            b = (-d - 1) % XN
            straight = send(stage.at[phase, pl.ds(a * ZN + first, count)], dst.at[pl.ds(b * ZN + first, count)], along_x(d))
            rows = pl.ds(0 if d == 1 else HALF, HALF)
            through = send(stage.at[phase, pl.ds(ZN + first, count), rows], transit.at[phase, 0 if d == 1 else 1, here], along_x(d))
            out.append((d, straight, through))
        return out

    def forward(phase, group, moves, dst):
        first, count = group
        out = []
        for d, straight, through in moves:
            through.wait_recv()
            rows = pl.ds(0 if d == 1 else HALF, HALF)
            out.append(send(transit.at[phase, 0 if d == 1 else 1, pl.ds(first, count)], dst.at[pl.ds(ZN + first, count), rows], along_x(d)))
        return out

    def arrive(moves, passed):
        for _, straight, _ in moves:
            straight.wait_recv()
        for copy in passed:
            copy.wait_recv()

    def choose(i, group):
        first, count = group
        for j in range(first, first + count):
            u = RANGE_AT[j]
            low, high = near[i][FAR + BLK_DEV * u], near[i][FAR + BLK_DEV * u + 1]
            for dx in range(1, XN):
                stage[i, (dx - 1) * ZN + j] = jnp.where(which_s[dx * ZN + u] == 1, high, low)

    pl.semaphore_wait(barrier, 4)

    top = ZN // 2
    moves = [[None] * len(GROUPS) for _ in range(4)]
    passed = [[None] * len(GROUPS) for _ in range(4)]

    def gather_x(i, t):
        choose(i, GROUPS[t])
        moves[i][t] = spread(i, GROUPS[t], near[i])

    def gather_on(i, t):
        passed[i][t] = forward(i, GROUPS[t], moves[i][t], near[i])

    rings = [None, None]

    def ring_step(i, t):
        for copy in rings[i]:
            copy.wait_recv()
        rings[i] = ring_send(i, t + 1) if t < top else None

    rings[0] = ring_send(0, 1)
    loads[0].wait()
    gather_x(0, 0)
    for t in range(1, top + 1):
        ring_step(0, t)
        gather_x(0, t)
        if t == 2:
            rings[1] = ring_send(1, 1)
        if t > 2:
            ring_step(1, t - 2)
        gather_on(0, t - 1)
    gather_on(0, top)
    ring_step(1, top - 1)
    loads[1].wait()
    for t in range(top):
        gather_x(1, t)
    ring_step(1, top)
    gather_x(1, top)
    loads[2].wait()
    loads[3].wait()
    for t in range(top + 1):
        arrive(moves[0][t], passed[0][t])

    def rows_of(s):
        return pl.ds(s * BLOCK, BLOCK)

    def fetch(i, b):
        full, turned = (k_s, kt_s) if i == 0 else (v_s, vt_s)
        for s in range(NSLOT):
            at = FAR + b if s == 0 else load_s[b * KSLOTS + s - 1]
            block = near[i][at]
            full[b, rows_of(s), :] = block
            turned[b, :, rows_of(s)] = block.T

    def bias(b, s):
        return jnp.where(s < kc[position * BLK_DEV + b], 0.0, NEG).astype(F32)

    def probs(b, pair):
        cols = pl.ds(pair * 2 * BLOCK, 2 * BLOCK)
        for h in (2 * pair, 2 * pair + 1):
            q_st[b, pl.ds(h * BLOCK, BLOCK), :] = q_in[b, :, pl.ds(h * DH, DH)]
            o_st[b, pl.ds(h * BLOCK, BLOCK), :] = o_in[b, :, pl.ds(h * DH, DH)]
        q2 = q_st[b, cols, :]
        m = None
        for s in range(NSLOT):
            sc = lax.dot_general(k_s[b, rows_of(s), :], q2, NT, preferred_element_type=F32)
            e_s[b, rows_of(s), cols] = sc
            high = jnp.max(sc, axis=0, keepdims=True)
            if s > 0:
                high = high + bias(b, s - 1)
            m = high if m is None else jnp.maximum(m, high)
        mc = m * SCALE2
        total = None
        for s in range(NSLOT):
            off = -mc if s == 0 else bias(b, s - 1) - mc
            e = jnp.exp2(e_s[b, rows_of(s), cols] * SCALE2 + off)
            e_s[b, rows_of(s), cols] = e
            part = jnp.sum(e, axis=0, keepdims=True)
            total = part if total is None else total + part
        inv = 1.0 / total
        inv_s[b, :, cols] = jnp.broadcast_to(inv, (8, 2 * BLOCK))
        for s in range(NSLOT):
            p_s[b, rows_of(s), cols] = (e_s[b, rows_of(s), cols] * inv).astype(BF16)

    def key_side(b, weights, rows_in, parts, own):
        for s in range(NSLOT):
            g = jnp.dot(weights[b, rows_of(s), :], rows_in[b], preferred_element_type=F32)
            if s == 0:
                own[b] = g
            else:
                parts[b * KSLOTS + s - 1] = g.astype(BF16)

    def query_side(b, pair):
        cols = pl.ds(pair * 2 * BLOCK, 2 * BLOCK)
        o2 = o_st[b, cols, :]
        out_t = jnp.dot(vt_s[b], p_s[b, :, cols], preferred_element_type=F32)
        att_t = out_t.astype(BF16)
        delta = jnp.sum(o2.T.astype(F32) * att_t.astype(F32), axis=0, keepdims=True)
        inv = inv_s[b, pl.ds(0, 1), cols] * SCALING
        for s in range(NSLOT):
            dp = lax.dot_general(v_s[b, rows_of(s), :], o2, NT, preferred_element_type=F32)
            ds_s[b, rows_of(s), cols] = ((e_s[b, rows_of(s), cols] * inv) * (dp - delta)).astype(BF16)
        gq_t = jnp.dot(kt_s[b], ds_s[b, :, cols], preferred_element_type=F32).astype(BF16)
        att, gq = att_t.T, gq_t.T
        for j in (0, 1):
            h = pl.ds((2 * pair + j) * DH, DH)
            att_s[b, :, h] = att[j * BLOCK:(j + 1) * BLOCK]
            gq_s[b, :, h] = gq[j * BLOCK:(j + 1) * BLOCK]

    parts = [parts_k, parts_v]

    def scatter_x(i, t):
        first, count = GROUPS[t]
        for j in range(first, first + count):
            for dx in range(1, XN):
                stage[2 + i, (dx - 1) * ZN + j] = parts[i][slot_s[dx * ZN + RANGE_AT[j]]]
        moves[2 + i][t] = spread(2 + i, GROUPS[t], terms.at[i])

    def scatter_on(i, t):
        passed[2 + i][t] = forward(2 + i, GROUPS[t], moves[2 + i][t], terms.at[i])

    def row_sums(i, t):
        arrive(moves[2 + i][t], passed[2 + i][t])
        first, count = GROUPS[t]
        for j in range(first, first + count):
            u = RANGE_AT[j]
            low = high = None
            for dx in range(XN):
                if dx == 0 and u == 0:
                    continue
                if dx == 0:
                    term = parts[i][slot_s[u]].astype(F32)
                else:
                    term = terms[i, (dx - 1) * ZN + j].astype(F32)
                second = which_s[dx * ZN + u] == 1
                up = jnp.where(second, term, 0.0)
                down = jnp.where(second, 0.0, term)
                high = up if high is None else high + up
                low = down if low is None else low + down
            rowsum[i, u, 0] = low.astype(BF16)
            rowsum[i, u, 1] = high.astype(BF16)

    chains = [None, None]

    def chain(i, t):
        out = []
        for j, d in enumerate((1, -1)):
            u = (-d * t) % ZN
            half = pl.ds(0 if d == 1 else 1, 1)
            if t == top:
                src, dst = rowsum.at[i, u, half], ring.at[i, j, t - 1, half]
            else:
                chains[i][j].wait_recv()
                for w in range(BLK_DEV):
                    if t + 1 < top or w == j:
                        both = rowsum[i, u, w].astype(F32) + ring[i, j, t, w].astype(F32)
                        rowsum[i, u, w] = both.astype(BF16)
                src, dst = rowsum.at[i, u], ring.at[i, j, t - 1]
            out.append(send(src, dst, along_z(-d)))
        chains[i] = out

    def finish(i):
        for copy in chains[i]:
            copy.wait_recv()
        own = (own_k, own_v)[i]
        out = (outk_ref, outv_ref)[i]
        for w in range(BLK_DEV):
            total = own[w] + rowsum[i, 0, w].astype(F32)
            total = total + ring[i, 0, 0, w].astype(F32) + ring[i, 1, 0, w].astype(F32)
            out[w] = total.astype(BF16)

    pairs = GROUP // 2
    units = [(b, pair) for b in range(BLK_DEV) for pair in range(pairs)]
    for i in (0, 1):
        parts[i][ENTRIES] = jnp.zeros((BLOCK, DH), BF16)
    for n, (b, pair) in enumerate(units):
        if pair == 0:
            fetch(0, b)
        probs(b, pair)
        if n <= top:
            gather_on(1, n)
        if pair == pairs - 1:
            key_side(b, p_s, o_st, parts_v, own_v)
    for t in range(top, -1, -1):
        scatter_x(1, t)
    for t in range(top + 1):
        arrive(moves[1][t], passed[1][t])
    stores = []
    for n, (b, pair) in enumerate(units):
        if pair == 0:
            fetch(1, b)
        query_side(b, pair)
        if n <= top:
            scatter_on(1, top - n)
        if n > 2:
            row_sums(1, top + 3 - n)
            if n - 3 < top:
                chain(1, top + 3 - n)
        if pair == pairs - 1:
            key_side(b, ds_s, q_st, parts_k, own_k)
            for src, dst in ((att_s, att_hbm), (gq_s, gq_hbm)):
                copy = pltpu.make_async_copy(src.at[b], dst.at[b], local_sem.at[4 + len(stores)])
                copy.start()
                stores.append(copy)
    for t in range(top, -1, -1):
        scatter_x(0, t)
    done = len(units) - 3
    for t in range(top, -1, -1):
        scatter_on(0, t)
        if top - t >= done:
            row_sums(1, t)
    for t in range(top - done, -1, -1):
        if t > 0 and top - t >= done:
            chain(1, t)
    for t in range(top, -1, -1):
        row_sums(0, t)
        if t > 0:
            chain(0, t)
    finish(1)
    finish(0)
    for copy in sent:
        copy.wait_send()
    for copy in stores:
        copy.wait()


def local(queries, keys, values, grad_out, key_blocks, key_count):
    rows, width = queries.shape
    wide = (BLK_DEV, BLOCK, width)
    own = (BLK_DEV, BLOCK, DH)
    any_spec = pl.BlockSpec(memory_space=pl.ANY)
    smem_spec = pl.BlockSpec(memory_space=pltpu.SMEM)
    vmem_spec = pl.BlockSpec(memory_space=pltpu.VMEM)
    vmem = pltpu.VMEM
    att, gq, gk, gv = pl.pallas_call(
        kernel,
        out_shape=[jax.ShapeDtypeStruct(wide, BF16)] * 2 + [jax.ShapeDtypeStruct(own, BF16)] * 2,
        in_specs=[smem_spec] * 2 + [any_spec] * 4,
        out_specs=[any_spec] * 2 + [vmem_spec] * 2,
        scratch_shapes=[
            vmem(wide, BF16), vmem(wide, BF16), vmem(wide, BF16), vmem(wide, BF16),
            vmem((FAR + BLK_DEV * ZN, BLOCK, DH), BF16), vmem((FAR + BLK_DEV * ZN, BLOCK, DH), BF16),
            vmem((4, FAR, BLOCK, DH), BF16), vmem((4, 2, ZN, HALF, DH), BF16), vmem((2, FAR, BLOCK, DH), BF16),
            vmem((2, 2, ZN // 2, BLK_DEV, BLOCK, DH), BF16), vmem((2, ZN, BLK_DEV, BLOCK, DH), BF16),
            vmem((ENTRIES + 1, BLOCK, DH), BF16), vmem((ENTRIES + 1, BLOCK, DH), BF16),
            vmem(own, F32), vmem(own, F32),
            vmem((BLK_DEV, WIDE, DH), BF16), vmem((BLK_DEV, WIDE, DH), BF16),
            vmem((BLK_DEV, DH, WIDE), BF16), vmem((BLK_DEV, DH, WIDE), BF16),
            vmem((BLK_DEV, GROUP * BLOCK, DH), BF16), vmem((BLK_DEV, GROUP * BLOCK, DH), BF16),
            vmem((BLK_DEV, WIDE, GROUP * BLOCK), F32),
            vmem((BLK_DEV, WIDE, GROUP * BLOCK), BF16), vmem((BLK_DEV, WIDE, GROUP * BLOCK), BF16),
            vmem((BLK_DEV, 8, GROUP * BLOCK), F32),
            pltpu.SMEM((XN * ZN,), jnp.int32), pltpu.SMEM((XN * ZN,), jnp.int32), pltpu.SMEM((ENTRIES,), jnp.int32),
            pltpu.SemaphoreType.DMA((COPIES,)), pltpu.SemaphoreType.DMA((COPIES,)), pltpu.SemaphoreType.DMA((8,))],
        compiler_params=pltpu.CompilerParams(collective_id=0, has_side_effects=True, vmem_limit_bytes=56 << 20),
        name="sparse_attention",
    )(key_blocks, key_count, queries.reshape(wide), grad_out.reshape(wide), keys.reshape(own), values.reshape(own))
    return att.reshape(rows, width), gq.reshape(rows, width), gk.reshape(rows, DH), gv.reshape(rows, DH)


def solution(mesh):
    in_specs = (P("ctx", "head"), P("ctx", "head"), P("ctx", "head"), P("ctx", "head"), P(), P())
    out_specs = (P("ctx", "head"), P("ctx", "head"), P("ctx", "head"), P("ctx", "head"))
    return jax.shard_map(local, mesh=mesh, in_specs=in_specs, out_specs=out_specs, check_vma=False)
```

```python
import functools
import math

import jax
import jax.numpy as jnp
from jax import lax
from jax.experimental import pallas as pl
from jax.experimental.pallas import tpu as pltpu
from jax.sharding import PartitionSpec as P

QH = 64
KVH = 8
DH = 128
BLOCK = 128
KSLOTS = 6
NSLOT = KSLOTS + 1
GROUP = QH // KVH
BLK_DEV = 2
ENTRIES = BLK_DEV * KSLOTS
XN = 4
ZN = 8
FAR = (XN - 1) * ZN
WIDE = NSLOT * BLOCK
SCALING = 1.0 / math.sqrt(DH)
SCALE2 = SCALING * 1.4426950408889634
NEG = -1e30
COPIES = 160
MESH = pl.DeviceIdType.MESH
BF16 = jnp.bfloat16
F32 = jnp.float32
NT = (((1,), (1,)), ((), ()))


def place(u):
    return 0 if u == 0 else (2 * u - 1 if u <= ZN // 2 else 2 * (ZN - u))


GROUPS = [(0, 1)] + [(2 * t - 1, 2) for t in range(1, ZN // 2)] + [(ZN - 1, 1)]
RANGE_AT = sorted(range(ZN), key=place)


def kernel(kb, kc, q_hbm, o_hbm, k_hbm, v_hbm, att_hbm, gq_hbm, outk_ref, outv_ref,
           q_in, o_in, att_s, gq_s, near_k, near_v, stage, terms, ring, rowsum,
           parts_k, parts_v, own_k, own_v, k_s, v_s, kt_s, vt_s, q_st, o_st, e_s, p_s, ds_s, dp_s, inv_s,
           which_s, slot_s, load_s, send_sem, recv_sem, local_sem):
    position = lax.axis_index("ctx")
    x = lax.rem(position, XN)
    z = lax.div(position, XN)
    near = [near_k, near_v]
    kv_hbm = [k_hbm, v_hbm]

    def along_x(dx):
        return z * XN + lax.rem(x + dx % XN, XN)

    def along_z(dz):
        return lax.rem(z + dz % ZN, ZN) * XN + x

    barrier = pltpu.get_barrier_semaphore()
    partners = [along_x(d) for d in range(1, XN)] + [along_z(d) for d in (1, -1, 2, -2)]
    for partner in partners:
        pl.semaphore_signal(barrier, inc=1, device_id={"ctx": partner}, device_id_type=MESH)

    loads = []
    for i, (src, dst) in enumerate((
            (k_hbm, near_k.at[pl.ds(FAR, BLK_DEV)]), (v_hbm, near_v.at[pl.ds(FAR, BLK_DEV)]),
            (q_hbm, q_in), (o_hbm, o_in))):
        copy = pltpu.make_async_copy(src, dst, local_sem.at[i])
        copy.start()
        loads.append(copy)

    for dx in range(XN):
        reader = along_x(dx) * BLK_DEV
        blocks, owners = [], []
        for e in range(ENTRIES):
            block = kb[reader + e // KSLOTS, e % KSLOTS]
            live = e % KSLOTS < kc[reader + e // KSLOTS]
            blocks.append(lax.rem(block, BLK_DEV))
            owners.append(jnp.where(live, lax.div(block, BLK_DEV), -1))
        for u in range(ZN):
            wanted = along_z(u)
            which = jnp.int32(0)
            for e in range(ENTRIES):
                which = jnp.where(owners[e] == wanted, blocks[e], which)
            which_s[dx * ZN + u] = which
        if dx == 0:
            for ax in range(XN):
                for u in range(ZN):
                    wanted = lax.rem(z + u, ZN) * XN + lax.rem(x + ax, XN)
                    slot = jnp.int32(ENTRIES)
                    for e in range(ENTRIES):
                        slot = jnp.where(owners[e] == wanted, e, slot)
                    slot_s[ax * ZN + u] = slot
    for b in range(BLK_DEV):
        block = position * BLK_DEV + b
        first = None
        for s in range(KSLOTS):
            listed = kb[block, s]
            owner = lax.div(listed, BLK_DEV)
            dx = lax.rem(lax.rem(owner, XN) - x + XN, XN)
            u = lax.rem(lax.div(owner, XN) - z + ZN, ZN)
            spot = jnp.where(u == 0, 0, jnp.where(u <= ZN // 2, 2 * u - 1, 2 * (ZN - u)))
            at = jnp.where(dx == 0, FAR + BLK_DEV * u + lax.rem(listed, BLK_DEV), (dx - 1) * ZN + spot)
            first = at if s == 0 else first
            load_s[b * KSLOTS + s] = jnp.where(s < kc[block], at, first)

    used = [0]
    sent = []

    def send(src, dst, device):
        at = used[0]
        used[0] += 1
        copy = pltpu.make_async_remote_copy(
            src_ref=src, dst_ref=dst, send_sem=send_sem.at[at], recv_sem=recv_sem.at[at],
            device_id={"ctx": device}, device_id_type=MESH)
        copy.start()
        sent.append(copy)
        return copy

    def column(i, u, half=None):
        first = FAR + BLK_DEV * (u % ZN)
        if half is None:
            return near[i].at[pl.ds(first, BLK_DEV)]
        return near[i].at[pl.ds(first + half, 1)]

    def ring_near(i):
        return {(t, d): send(kv_hbm[i], column(i, -d * t), along_z(d * t)) for t in (1, 2) for d in (1, -1)}

    def ring_far(i):
        out = {(3, d): send(column(i, -2 * d), column(i, -3 * d), along_z(d)) for d in (1, -1)}
        for half, d in enumerate((1, -1)):
            out[4, d] = send(column(i, -2 * d, half), column(i, 4, half), along_z(2 * d))
        return out

    def spread(phase, group, dst):
        first, count = group
        return [send(stage.at[phase, pl.ds((dx - 1) * ZN + first, count)],
                     dst.at[pl.ds((XN - dx - 1) * ZN + first, count)], along_x(dx)) for dx in (2, 1, 3)]

    def arrive(copies):
        for copy in copies:
            copy.wait_recv()

    def choose(i, group):
        first, count = group
        for j in range(first, first + count):
            u = RANGE_AT[j]
            low, high = near[i][FAR + BLK_DEV * u], near[i][FAR + BLK_DEV * u + 1]
            for dx in range(1, XN):
                stage[i, (dx - 1) * ZN + j] = jnp.where(which_s[dx * ZN + u] == 1, high, low)

    pl.semaphore_wait(barrier, len(partners))

    top = ZN // 2
    moves = [[None] * len(GROUPS) for _ in range(4)]
    rings = [{}, {}]

    def gather_x(i, t):
        choose(i, GROUPS[t])
        moves[i][t] = spread(i, GROUPS[t], near[i])

    def come(i, t):
        for d in (1, -1):
            rings[i][t, d].wait_recv()

    rings[0].update(ring_near(0))
    loads[0].wait()
    gather_x(0, 0)
    rings[1].update(ring_near(1))
    come(0, 1)
    gather_x(0, 1)
    come(0, 2)
    rings[0].update(ring_far(0))
    gather_x(0, 2)
    loads[1].wait()
    gather_x(1, 0)
    come(1, 1)
    gather_x(1, 1)
    come(1, 2)
    rings[1].update(ring_far(1))
    come(0, 3)
    gather_x(0, 3)
    come(0, 4)
    gather_x(0, 4)
    gather_x(1, 2)
    come(1, 3)
    gather_x(1, 3)
    come(1, 4)
    gather_x(1, 4)
    loads[2].wait()
    loads[3].wait()
    for t in range(top + 1):
        arrive(moves[0][t])

    def rows_of(s):
        return pl.ds(s * BLOCK, BLOCK)

    def fetch(i, b):
        full, turned = (k_s, kt_s) if i == 0 else (v_s, vt_s)
        for s in range(NSLOT):
            at = FAR + b if s == 0 else load_s[b * KSLOTS + s - 1]
            block = near[i][at]
            full[b, rows_of(s), :] = block
            turned[b, :, rows_of(s)] = block.T

    def bias(b, s):
        return jnp.where(s < kc[position * BLK_DEV + b], 0.0, NEG).astype(F32)

    def probs(b, pair):
        cols = pl.ds(pair * 2 * BLOCK, 2 * BLOCK)
        for h in (2 * pair, 2 * pair + 1):
            q_st[b, pl.ds(h * BLOCK, BLOCK), :] = q_in[b, :, pl.ds(h * DH, DH)]
            o_st[b, pl.ds(h * BLOCK, BLOCK), :] = o_in[b, :, pl.ds(h * DH, DH)]
        q2 = q_st[b, cols, :]
        m = None
        e_s[b, :, cols] = lax.dot_general(k_s[b], q2, NT, preferred_element_type=F32)
        for s in range(NSLOT):
            high = jnp.max(e_s[b, rows_of(s), cols], axis=0, keepdims=True)
            if s > 0:
                high = high + bias(b, s - 1)
            m = high if m is None else jnp.maximum(m, high)
        mc = m * SCALE2
        total = None
        for s in range(NSLOT):
            off = -mc if s == 0 else bias(b, s - 1) - mc
            e = jnp.exp2(e_s[b, rows_of(s), cols] * SCALE2 + off)
            e_s[b, rows_of(s), cols] = e
            part = jnp.sum(e, axis=0, keepdims=True)
            total = part if total is None else total + part
        inv = 1.0 / total
        inv_s[b, :, cols] = jnp.broadcast_to(inv, (8, 2 * BLOCK))
        for s in range(NSLOT):
            p_s[b, rows_of(s), cols] = (e_s[b, rows_of(s), cols] * inv).astype(BF16)

    def key_side(b, weights, rows_in, parts, own):
        g = jnp.dot(weights[b], rows_in[b], preferred_element_type=F32)
        own[b] = g[:BLOCK]
        for s in range(KSLOTS):
            parts[b * KSLOTS + s] = g[(s + 1) * BLOCK:(s + 2) * BLOCK].astype(BF16)

    def query_side(b, pair):
        cols = pl.ds(pair * 2 * BLOCK, 2 * BLOCK)
        o2 = o_st[b, cols, :]
        dp_s[...] = lax.dot_general(v_s[b], o2, NT, preferred_element_type=F32)
        out_t = jnp.dot(vt_s[b], p_s[b, :, cols], preferred_element_type=F32)
        att_t = out_t.astype(BF16)
        delta = jnp.sum(o2.T.astype(F32) * att_t.astype(F32), axis=0, keepdims=True)
        inv = inv_s[b, pl.ds(0, 1), cols] * SCALING
        for s in range(NSLOT):
            dp = dp_s[rows_of(s), :]
            ds_s[b, rows_of(s), cols] = ((e_s[b, rows_of(s), cols] * inv) * (dp - delta)).astype(BF16)
        gq_t = jnp.dot(kt_s[b], ds_s[b, :, cols], preferred_element_type=F32).astype(BF16)
        att, gq = att_t.T, gq_t.T
        for j in (0, 1):
            h = pl.ds((2 * pair + j) * DH, DH)
            att_s[b, :, h] = att[j * BLOCK:(j + 1) * BLOCK]
            gq_s[b, :, h] = gq[j * BLOCK:(j + 1) * BLOCK]

    parts = [parts_k, parts_v]

    def scatter_x(i, t):
        first, count = GROUPS[t]
        for j in range(first, first + count):
            for dx in range(1, XN):
                stage[2 + i, (dx - 1) * ZN + j] = parts[i][slot_s[dx * ZN + RANGE_AT[j]]]
        moves[2 + i][t] = spread(2 + i, GROUPS[t], terms.at[i])

    def row_sums(i, t):
        arrive(moves[2 + i][t])
        first, count = GROUPS[t]
        for j in range(first, first + count):
            u = RANGE_AT[j]
            low = high = None
            for dx in range(XN):
                if dx == 0 and u == 0:
                    continue
                if dx == 0:
                    term = parts[i][slot_s[u]].astype(F32)
                else:
                    term = terms[i, (dx - 1) * ZN + j].astype(F32)
                second = which_s[dx * ZN + u] == 1
                up = jnp.where(second, term, 0.0)
                down = jnp.where(second, 0.0, term)
                high = up if high is None else high + up
                low = down if low is None else low + down
            rowsum[i, u, 0] = low.astype(BF16)
            rowsum[i, u, 1] = high.astype(BF16)

    chains = [{}, {}]

    def chain(i, t):
        for j, d in enumerate((1, -1)):
            u = (-d * t) % ZN
            dst = ring.at[i, j, t - 1]
            src = rowsum.at[i, u]
            if t == 4:
                src, dst = src.at[pl.ds(j, 1)], dst.at[pl.ds(j, 1)]
            if t == 2:
                chains[i][3, d].wait_recv()
                chains[i][4, d].wait_recv()
                for w in range(BLK_DEV):
                    both = rowsum[i, u, w].astype(F32) + ring[i, j, 2, w].astype(F32)
                    if w == j:
                        both = both + ring[i, j, 3, w].astype(F32)
                    rowsum[i, u, w] = both.astype(BF16)
            chains[i][t, d] = send(src, dst, along_z(-d * t if t < 3 else (2 - t) * d))

    def finish(i):
        for t in (1, 2):
            for d in (1, -1):
                chains[i][t, d].wait_recv()
        own = (own_k, own_v)[i]
        out = (outk_ref, outv_ref)[i]
        for w in range(BLK_DEV):
            total = own[w] + rowsum[i, 0, w].astype(F32)
            for t in (1, 2):
                for j in (0, 1):
                    total = total + ring[i, j, t - 1, w].astype(F32)
            out[w] = total.astype(BF16)

    pairs = GROUP // 2
    units = [(b, pair) for b in range(BLK_DEV) for pair in range(pairs)]
    for i in (0, 1):
        parts[i][ENTRIES] = jnp.zeros((BLOCK, DH), BF16)
    for b, pair in units:
        if pair == 0:
            fetch(0, b)
        probs(b, pair)
        if pair == pairs - 1:
            key_side(b, p_s, o_st, parts_v, own_v)
    for t in range(top, -1, -1):
        scatter_x(1, t)
    for t in range(top + 1):
        arrive(moves[1][t])
    stores = []

    def sums_on(i, t):
        row_sums(i, t)
        if t in (4, 3, 1):
            chain(i, t)
        if t == 1:
            chain(i, 2)

    for n, (b, pair) in enumerate(units):
        if pair == 0:
            fetch(1, b)
        query_side(b, pair)
        if n > 2:
            sums_on(1, top + 3 - n)
        if pair == pairs - 1:
            key_side(b, ds_s, q_st, parts_k, own_k)
            for src, dst in ((att_s, att_hbm), (gq_s, gq_hbm)):
                copy = pltpu.make_async_copy(src.at[b], dst.at[b], local_sem.at[4 + len(stores)])
                copy.start()
                stores.append(copy)
    for t in range(top, -1, -1):
        scatter_x(0, t)
    for t in range(top, -1, -1):
        sums_on(0, t)
    finish(1)
    finish(0)
    for copy in sent:
        copy.wait_send()
    for copy in stores:
        copy.wait()


def local(queries, keys, values, grad_out, key_blocks, key_count):
    rows, width = queries.shape
    wide = (BLK_DEV, BLOCK, width)
    own = (BLK_DEV, BLOCK, DH)
    any_spec = pl.BlockSpec(memory_space=pl.ANY)
    smem_spec = pl.BlockSpec(memory_space=pltpu.SMEM)
    vmem_spec = pl.BlockSpec(memory_space=pltpu.VMEM)
    vmem = pltpu.VMEM
    att, gq, gk, gv = pl.pallas_call(
        kernel,
        out_shape=[jax.ShapeDtypeStruct(wide, BF16)] * 2 + [jax.ShapeDtypeStruct(own, BF16)] * 2,
        in_specs=[smem_spec] * 2 + [any_spec] * 4,
        out_specs=[any_spec] * 2 + [vmem_spec] * 2,
        scratch_shapes=[
            vmem(wide, BF16), vmem(wide, BF16), vmem(wide, BF16), vmem(wide, BF16),
            vmem((FAR + BLK_DEV * ZN, BLOCK, DH), BF16), vmem((FAR + BLK_DEV * ZN, BLOCK, DH), BF16),
            vmem((4, FAR, BLOCK, DH), BF16), vmem((2, FAR, BLOCK, DH), BF16),
            vmem((2, 2, ZN // 2, BLK_DEV, BLOCK, DH), BF16), vmem((2, ZN, BLK_DEV, BLOCK, DH), BF16),
            vmem((ENTRIES + 1, BLOCK, DH), BF16), vmem((ENTRIES + 1, BLOCK, DH), BF16),
            vmem(own, F32), vmem(own, F32),
            vmem((BLK_DEV, WIDE, DH), BF16), vmem((BLK_DEV, WIDE, DH), BF16),
            vmem((BLK_DEV, DH, WIDE), BF16), vmem((BLK_DEV, DH, WIDE), BF16),
            vmem((BLK_DEV, GROUP * BLOCK, DH), BF16), vmem((BLK_DEV, GROUP * BLOCK, DH), BF16),
            vmem((BLK_DEV, WIDE, GROUP * BLOCK), F32),
            vmem((BLK_DEV, WIDE, GROUP * BLOCK), BF16), vmem((BLK_DEV, WIDE, GROUP * BLOCK), BF16),
            vmem((WIDE, 2 * BLOCK), F32), vmem((BLK_DEV, 8, GROUP * BLOCK), F32),
            pltpu.SMEM((XN * ZN,), jnp.int32), pltpu.SMEM((XN * ZN,), jnp.int32), pltpu.SMEM((ENTRIES,), jnp.int32),
            pltpu.SemaphoreType.DMA((COPIES,)), pltpu.SemaphoreType.DMA((COPIES,)), pltpu.SemaphoreType.DMA((8,))],
        compiler_params=pltpu.CompilerParams(collective_id=0, has_side_effects=True, vmem_limit_bytes=56 << 20),
        name="sparse_attention",
    )(key_blocks, key_count, queries.reshape(wide), grad_out.reshape(wide), keys.reshape(own), values.reshape(own))
    return att.reshape(rows, width), gq.reshape(rows, width), gk.reshape(rows, DH), gv.reshape(rows, DH)


def solution(mesh):
    in_specs = (P("ctx", "head"), P("ctx", "head"), P("ctx", "head"), P("ctx", "head"), P(), P())
    out_specs = (P("ctx", "head"), P("ctx", "head"), P("ctx", "head"), P("ctx", "head"))
    return jax.shard_map(local, mesh=mesh, in_specs=in_specs, out_specs=out_specs, check_vma=False)
```

```python
import functools
import math

import jax
import jax.numpy as jnp
from jax import lax
from jax.experimental import pallas as pl
from jax.experimental.pallas import tpu as pltpu
from jax.sharding import PartitionSpec as P

QH = 64
KVH = 8
DH = 128
BLOCK = 128
KSLOTS = 6
NSLOT = KSLOTS + 1
GROUP = QH // KVH
BLK_DEV = 2
ENTRIES = BLK_DEV * KSLOTS
XN = 4
ZN = 8
FAR = (XN - 1) * ZN
WIDE = NSLOT * BLOCK
SCALING = 1.0 / math.sqrt(DH)
SCALE2 = SCALING * 1.4426950408889634
NEG = -1e30
SENDS = 8
RECVS = 44
MESH = pl.DeviceIdType.MESH
BF16 = jnp.bfloat16
F32 = jnp.float32
NT = (((1,), (1,)), ((), ()))


def place(u):
    return 0 if u == 0 else (2 * u - 1 if u <= ZN // 2 else 2 * (ZN - u))


GROUPS = [(0, 1)] + [(2 * t - 1, 2) for t in range(1, ZN // 2)] + [(ZN - 1, 1)]
RANGE_AT = sorted(range(ZN), key=place)


def kernel(kb, kc, q_hbm, o_hbm, k_hbm, v_hbm, att_hbm, gq_hbm, outk_ref, outv_ref,
           q_in, o_in, att_s, gq_s, near_k, near_v, stage, terms, ring, rowsum,
           parts_k, parts_v, own_k, own_v, k_s, v_s, kt_s, vt_s, q_st, o_st, e_s, p_s, ds_s, dp_s, inv_s,
           which_s, slot_s, load_s, send_sem, recv_sem, local_sem):
    position = lax.axis_index("ctx")
    x = lax.rem(position, XN)
    z = lax.div(position, XN)
    near = [near_k, near_v]
    kv_hbm = [k_hbm, v_hbm]

    def along_x(dx):
        return z * XN + lax.rem(x + dx % XN, XN)

    def along_z(dz):
        return lax.rem(z + dz % ZN, ZN) * XN + x

    barrier = pltpu.get_barrier_semaphore()
    partners = [along_x(d) for d in range(1, XN)] + [along_z(d) for d in (1, -1, 2, -2)]
    for partner in partners:
        pl.semaphore_signal(barrier, inc=1, device_id={"ctx": partner}, device_id_type=MESH)

    loads = []
    for i, (src, dst) in enumerate((
            (k_hbm, near_k.at[pl.ds(FAR, BLK_DEV)]), (v_hbm, near_v.at[pl.ds(FAR, BLK_DEV)]),
            (q_hbm, q_in), (o_hbm, o_in))):
        copy = pltpu.make_async_copy(src, dst, local_sem.at[i])
        copy.start()
        loads.append(copy)

    for dx in range(XN):
        reader = along_x(dx) * BLK_DEV
        blocks, owners = [], []
        for e in range(ENTRIES):
            block = kb[e % KSLOTS, reader + e // KSLOTS]
            live = e % KSLOTS < kc[reader + e // KSLOTS]
            blocks.append(lax.rem(block, BLK_DEV))
            owners.append(jnp.where(live, lax.div(block, BLK_DEV), -1))
        for u in range(ZN):
            wanted = along_z(u)
            which = jnp.int32(0)
            for e in range(ENTRIES):
                which = jnp.where(owners[e] == wanted, blocks[e], which)
            which_s[dx * ZN + u] = which
        if dx == 0:
            for ax in range(XN):
                for u in range(ZN):
                    wanted = lax.rem(z + u, ZN) * XN + lax.rem(x + ax, XN)
                    slot = jnp.int32(ENTRIES)
                    for e in range(ENTRIES):
                        slot = jnp.where(owners[e] == wanted, e, slot)
                    slot_s[ax * ZN + u] = slot
    for b in range(BLK_DEV):
        block = position * BLK_DEV + b
        first = None
        for s in range(KSLOTS):
            listed = kb[s, block]
            owner = lax.div(listed, BLK_DEV)
            dx = lax.rem(lax.rem(owner, XN) - x + XN, XN)
            u = lax.rem(lax.div(owner, XN) - z + ZN, ZN)
            spot = jnp.where(u == 0, 0, jnp.where(u <= ZN // 2, 2 * u - 1, 2 * (ZN - u)))
            at = jnp.where(dx == 0, FAR + BLK_DEV * u + lax.rem(listed, BLK_DEV), (dx - 1) * ZN + spot)
            first = at if s == 0 else first
            load_s[b * KSLOTS + s] = jnp.where(s < kc[block], at, first)

    used = [0]

    def fresh():
        used[0] += 1
        return used[0] - 1

    def send(src, dst, device, out, at):
        copy = pltpu.make_async_remote_copy(
            src_ref=src, dst_ref=dst, send_sem=send_sem.at[out], recv_sem=recv_sem.at[at],
            device_id={"ctx": device}, device_id_type=MESH)
        copy.start()
        return copy

    def wait_sent(ref, out):
        pltpu.make_async_remote_copy(
            src_ref=ref, dst_ref=ref, send_sem=send_sem.at[out], recv_sem=recv_sem.at[0],
            device_id={"ctx": partners[0]}, device_id_type=MESH).wait_send()

    def wait_come(ref, at):
        pltpu.make_async_remote_copy(
            src_ref=ref, dst_ref=ref, send_sem=send_sem.at[0], recv_sem=recv_sem.at[at],
            device_id={"ctx": partners[0]}, device_id_type=MESH).wait_recv()

    def column(i, u, half=None):
        first = FAR + BLK_DEV * (u % ZN)
        if half is None:
            return near[i].at[pl.ds(first, BLK_DEV)]
        return near[i].at[pl.ds(first + half, 1)]

    def ring_near(i):
        return {(t, d): send(kv_hbm[i], column(i, -d * t), along_z(d * t), i, fresh()) for t in (1, 2) for d in (1, -1)}

    def ring_far(i):
        out = {(3, d): send(column(i, -2 * d), column(i, -3 * d), along_z(d), i, fresh()) for d in (1, -1)}
        for half, d in enumerate((1, -1)):
            out[4, d] = send(column(i, -2 * d, half), column(i, 4, half), along_z(2 * d), i, fresh())
        return out

    def spread(phase, group, dst_at, at):
        first, count = group
        for dx in (2, 1, 3):
            send(stage.at[phase, pl.ds((dx - 1) * ZN + first, count)], dst_at(XN - dx, first, count), along_x(dx), 4 + phase, at)

    def choose(i, group):
        first, count = group
        for j in range(first, first + count):
            u = RANGE_AT[j]
            low, high = near[i][FAR + BLK_DEV * u], near[i][FAR + BLK_DEV * u + 1]
            for dx in range(1, XN):
                stage[i, (dx - 1) * ZN + j] = jnp.where(which_s[dx * ZN + u] == 1, high, low)

    pl.semaphore_wait(barrier, len(partners))

    top = ZN // 2
    far_come = [fresh(), fresh()]
    rings = [{}, {}]

    def gather_x(i, t):
        choose(i, GROUPS[t])
        spread(i, GROUPS[t], lambda dx, first, count: near[i].at[pl.ds((dx - 1) * ZN + first, count)], far_come[i])

    def come(i, t):
        for d in (1, -1):
            rings[i][t, d].wait_recv()

    rings[0].update(ring_near(0))
    loads[0].wait()
    gather_x(0, 0)
    rings[1].update(ring_near(1))
    come(0, 1)
    gather_x(0, 1)
    come(0, 2)
    rings[0].update(ring_far(0))
    gather_x(0, 2)
    loads[1].wait()
    gather_x(1, 0)
    come(1, 1)
    gather_x(1, 1)
    come(1, 2)
    rings[1].update(ring_far(1))
    come(0, 3)
    gather_x(0, 3)
    come(0, 4)
    gather_x(0, 4)
    gather_x(1, 2)
    come(1, 3)
    gather_x(1, 3)
    come(1, 4)
    gather_x(1, 4)
    loads[2].wait()
    loads[3].wait()
    wait_come(near[0].at[pl.ds(0, FAR)], far_come[0])

    def rows_of(s):
        return pl.ds(s * BLOCK, BLOCK)

    def fetch(i, b):
        full, turned = (k_s, kt_s) if i == 0 else (v_s, vt_s)
        for s in range(NSLOT):
            at = FAR + b if s == 0 else load_s[b * KSLOTS + s - 1]
            block = near[i][at]
            full[b, rows_of(s), :] = block
            turned[b, :, rows_of(s)] = block.T

    def bias(b, s):
        return jnp.where(s < kc[position * BLK_DEV + b], 0.0, NEG).astype(F32)

    def probs(b, pair):
        cols = pl.ds(pair * 2 * BLOCK, 2 * BLOCK)
        for h in (2 * pair, 2 * pair + 1):
            q_st[b, pl.ds(h * BLOCK, BLOCK), :] = q_in[b, :, pl.ds(h * DH, DH)]
            o_st[b, pl.ds(h * BLOCK, BLOCK), :] = o_in[b, :, pl.ds(h * DH, DH)]
        q2 = q_st[b, cols, :]
        m = None
        e_s[b, :, cols] = lax.dot_general(k_s[b], q2, NT, preferred_element_type=F32)
        for s in range(NSLOT):
            high = jnp.max(e_s[b, rows_of(s), cols], axis=0, keepdims=True)
            if s > 0:
                high = high + bias(b, s - 1)
            m = high if m is None else jnp.maximum(m, high)
        mc = m * SCALE2
        total = None
        for s in range(NSLOT):
            off = -mc if s == 0 else bias(b, s - 1) - mc
            e = jnp.exp2(e_s[b, rows_of(s), cols] * SCALE2 + off)
            e_s[b, rows_of(s), cols] = e
            part = jnp.sum(e, axis=0, keepdims=True)
            total = part if total is None else total + part
        inv = 1.0 / total
        inv_s[b, :, cols] = jnp.broadcast_to(inv, (8, 2 * BLOCK))
        for s in range(NSLOT):
            p_s[b, rows_of(s), cols] = (e_s[b, rows_of(s), cols] * inv).astype(BF16)

    def key_side(b, weights, rows_in, parts, own):
        g = jnp.dot(weights[b], rows_in[b], preferred_element_type=F32)
        own[b] = g[:BLOCK]
        for s in range(KSLOTS):
            parts[b * KSLOTS + s] = g[(s + 1) * BLOCK:(s + 2) * BLOCK].astype(BF16)

    def query_side(b, pair):
        cols = pl.ds(pair * 2 * BLOCK, 2 * BLOCK)
        o2 = o_st[b, cols, :]
        dp_s[...] = lax.dot_general(v_s[b], o2, NT, preferred_element_type=F32)
        out_t = jnp.dot(vt_s[b], p_s[b, :, cols], preferred_element_type=F32)
        att_t = out_t.astype(BF16)
        delta = jnp.sum(o2.T.astype(F32) * att_t.astype(F32), axis=0, keepdims=True)
        inv = inv_s[b, pl.ds(0, 1), cols] * SCALING
        for s in range(NSLOT):
            dp = dp_s[rows_of(s), :]
            ds_s[b, rows_of(s), cols] = ((e_s[b, rows_of(s), cols] * inv) * (dp - delta)).astype(BF16)
        gq_t = jnp.dot(kt_s[b], ds_s[b, :, cols], preferred_element_type=F32).astype(BF16)
        att, gq = att_t.T, gq_t.T
        for j in (0, 1):
            h = pl.ds((2 * pair + j) * DH, DH)
            att_s[b, :, h] = att[j * BLOCK:(j + 1) * BLOCK]
            gq_s[b, :, h] = gq[j * BLOCK:(j + 1) * BLOCK]

    parts = [parts_k, parts_v]

    terms_come = {}

    def scatter_x(i, t):
        first, count = GROUPS[t]
        for j in range(first, first + count):
            for dx in range(1, XN):
                stage[2 + i, (dx - 1) * ZN + j] = parts[i][slot_s[dx * ZN + RANGE_AT[j]]]
        terms_come[i, t] = fresh()
        spread(2 + i, GROUPS[t], lambda dx, first, count: terms.at[i, pl.ds(first, count), dx - 1], terms_come[i, t])

    def row_sums(i, t):
        first, count = GROUPS[t]
        wait_come(terms.at[i, pl.ds(first, count)], terms_come[i, t])
        for j in range(first, first + count):
            u = RANGE_AT[j]
            low = high = None
            for dx in range(XN):
                if dx == 0 and u == 0:
                    continue
                if dx == 0:
                    term = parts[i][slot_s[u]].astype(F32)
                else:
                    term = terms[i, j, dx - 1].astype(F32)
                second = which_s[dx * ZN + u] == 1
                up = jnp.where(second, term, 0.0)
                down = jnp.where(second, 0.0, term)
                high = up if high is None else high + up
                low = down if low is None else low + down
            rowsum[i, u, 0] = low.astype(BF16)
            rowsum[i, u, 1] = high.astype(BF16)

    chains = [{}, {}]

    def chain(i, t):
        for j, d in enumerate((1, -1)):
            u = (-d * t) % ZN
            dst = ring.at[i, j, t - 1]
            src = rowsum.at[i, u]
            if t == 4:
                src, dst = src.at[pl.ds(j, 1)], dst.at[pl.ds(j, 1)]
            if t == 2:
                chains[i][3, d].wait_recv()
                chains[i][4, d].wait_recv()
                for w in range(BLK_DEV):
                    both = rowsum[i, u, w].astype(F32) + ring[i, j, 2, w].astype(F32)
                    if w == j:
                        both = both + ring[i, j, 3, w].astype(F32)
                    rowsum[i, u, w] = both.astype(BF16)
            chains[i][t, d] = send(src, dst, along_z(-d * t if t < 3 else (2 - t) * d), 2 + i, fresh())

    def finish(i):
        for t in (1, 2):
            for d in (1, -1):
                chains[i][t, d].wait_recv()
        own = (own_k, own_v)[i]
        out = (outk_ref, outv_ref)[i]
        for w in range(BLK_DEV):
            total = own[w] + rowsum[i, 0, w].astype(F32)
            for t in (1, 2):
                for j in (0, 1):
                    total = total + ring[i, j, t - 1, w].astype(F32)
            out[w] = total.astype(BF16)

    pairs = GROUP // 2
    units = [(b, pair) for b in range(BLK_DEV) for pair in range(pairs)]
    for i in (0, 1):
        parts[i][ENTRIES] = jnp.zeros((BLOCK, DH), BF16)
    for b, pair in units:
        if pair == 0:
            fetch(0, b)
        probs(b, pair)
        if pair == pairs - 1:
            key_side(b, p_s, o_st, parts_v, own_v)
    for t in range(top, -1, -1):
        scatter_x(1, t)
    wait_come(near[1].at[pl.ds(0, FAR)], far_come[1])
    stores = []

    def sums_on(i, t):
        row_sums(i, t)
        if t in (4, 3, 1):
            chain(i, t)
        if t == 1:
            chain(i, 2)

    for n, (b, pair) in enumerate(units):
        if pair == 0:
            fetch(1, b)
        query_side(b, pair)
        if n > 2:
            sums_on(1, top + 3 - n)
        if pair == pairs - 1:
            key_side(b, ds_s, q_st, parts_k, own_k)
            for src, dst in ((att_s, att_hbm), (gq_s, gq_hbm)):
                copy = pltpu.make_async_copy(src.at[b], dst.at[b], local_sem.at[4 + len(stores)])
                copy.start()
                stores.append(copy)
    for t in range(top, -1, -1):
        scatter_x(0, t)
    for t in range(top, -1, -1):
        sums_on(0, t)
    finish(1)
    finish(0)
    for i in (0, 1):
        ring_bytes = near[i].at[pl.ds(0, 7 * BLK_DEV)]
        wait_sent(ring_bytes, i)
        wait_sent(ring_bytes, 2 + i)
    for phase in range(4):
        wait_sent(stage.at[phase], 4 + phase)
    for copy in stores:
        copy.wait()


def hand_on(*refs):
    inputs, outputs, held, sems = refs[:4], refs[4:8], refs[8:12], refs[12]
    parts = [(i, pl.ds(p * BLOCK, BLOCK)) for i in range(4) for p in range(BLK_DEV)]
    reads = [pltpu.make_async_copy(inputs[i].at[rows], held[i].at[rows], sems.at[0, n]) for n, (i, rows) in enumerate(parts)]
    writes = [pltpu.make_async_copy(held[i].at[rows], outputs[i].at[rows], sems.at[1, n]) for n, (i, rows) in enumerate(parts)]
    for copy in reads:
        copy.start()
    for read, write in zip(reads, writes):
        read.wait()
        write.start()
    for copy in writes:
        copy.wait()


def local(queries, keys, values, grad_out, key_blocks, key_count):
    rows, width = queries.shape
    wide = (BLK_DEV, BLOCK, width)
    own = (BLK_DEV, BLOCK, DH)
    any_spec = pl.BlockSpec(memory_space=pl.ANY)
    smem_spec = pl.BlockSpec(memory_space=pltpu.SMEM)
    vmem_spec = pl.BlockSpec(memory_space=pltpu.VMEM)
    vmem = pltpu.VMEM
    att, gq, gk, gv = pl.pallas_call(
        kernel,
        out_shape=[jax.ShapeDtypeStruct(wide, BF16)] * 2 + [jax.ShapeDtypeStruct(own, BF16)] * 2,
        in_specs=[smem_spec] * 2 + [any_spec] * 4,
        out_specs=[any_spec] * 2 + [vmem_spec] * 2,
        scratch_shapes=[
            vmem(wide, BF16), vmem(wide, BF16), vmem(wide, BF16), vmem(wide, BF16),
            vmem((FAR + BLK_DEV * ZN, BLOCK, DH), BF16), vmem((FAR + BLK_DEV * ZN, BLOCK, DH), BF16),
            vmem((4, FAR, BLOCK, DH), BF16), vmem((2, ZN, XN - 1, BLOCK, DH), BF16),
            vmem((2, 2, ZN // 2, BLK_DEV, BLOCK, DH), BF16), vmem((2, ZN, BLK_DEV, BLOCK, DH), BF16),
            vmem((ENTRIES + 1, BLOCK, DH), BF16), vmem((ENTRIES + 1, BLOCK, DH), BF16),
            vmem(own, F32), vmem(own, F32),
            vmem((BLK_DEV, WIDE, DH), BF16), vmem((BLK_DEV, WIDE, DH), BF16),
            vmem((BLK_DEV, DH, WIDE), BF16), vmem((BLK_DEV, DH, WIDE), BF16),
            vmem((BLK_DEV, GROUP * BLOCK, DH), BF16), vmem((BLK_DEV, GROUP * BLOCK, DH), BF16),
            vmem((BLK_DEV, WIDE, GROUP * BLOCK), F32),
            vmem((BLK_DEV, WIDE, GROUP * BLOCK), BF16), vmem((BLK_DEV, WIDE, GROUP * BLOCK), BF16),
            vmem((WIDE, 2 * BLOCK), F32), vmem((BLK_DEV, 8, GROUP * BLOCK), F32),
            pltpu.SMEM((XN * ZN,), jnp.int32), pltpu.SMEM((XN * ZN,), jnp.int32), pltpu.SMEM((ENTRIES,), jnp.int32),
            pltpu.SemaphoreType.DMA((SENDS,)), pltpu.SemaphoreType.DMA((RECVS,)), pltpu.SemaphoreType.DMA((8,))],
        compiler_params=pltpu.CompilerParams(collective_id=0, has_side_effects=True, vmem_limit_bytes=56 << 20),
        name="sparse_attention",
    )(key_blocks.T, key_count, queries.reshape(wide), grad_out.reshape(wide), keys.reshape(own), values.reshape(own))
    results = [att.reshape(rows, width), gq.reshape(rows, width), gk.reshape(rows, DH), gv.reshape(rows, DH)]
    return tuple(pl.pallas_call(
        hand_on,
        out_shape=[jax.ShapeDtypeStruct(a.shape, a.dtype) for a in results],
        in_specs=[any_spec] * 4,
        out_specs=[any_spec] * 4,
        scratch_shapes=[vmem(a.shape, a.dtype) for a in results] + [pltpu.SemaphoreType.DMA((2, 4 * BLK_DEV))],
        name="hand_on",
    )(*results))


def solution(mesh):
    in_specs = (P("ctx", "head"), P("ctx", "head"), P("ctx", "head"), P("ctx", "head"), P(), P())
    out_specs = (P("ctx", "head"), P("ctx", "head"), P("ctx", "head"), P("ctx", "head"))
    return jax.shard_map(local, mesh=mesh, in_specs=in_specs, out_specs=out_specs, check_vma=False)
```

```python
import functools
import math

import jax
import jax.numpy as jnp
from jax import lax
from jax.experimental import pallas as pl
from jax.experimental.pallas import tpu as pltpu
from jax.sharding import PartitionSpec as P

QH = 64
KVH = 8
DH = 128
BLOCK = 128
KSLOTS = 6
NSLOT = KSLOTS + 1
GROUP = QH // KVH
BLK_DEV = 2
ENTRIES = BLK_DEV * KSLOTS
XN = 4
ZN = 8
FAR = (XN - 1) * ZN
WIDE = NSLOT * BLOCK
SCALING = 1.0 / math.sqrt(DH)
SCALE2 = SCALING * 1.4426950408889634
NEG = -1e30
SENDS = 20
RECVS = 64
CUT = 80
REST = BLOCK - CUT
MESH = pl.DeviceIdType.MESH
BF16 = jnp.bfloat16
F32 = jnp.float32
NT = (((1,), (1,)), ((), ()))


def place(u):
    return 0 if u == 0 else (2 * u - 1 if u <= ZN // 2 else 2 * (ZN - u))


def base(dx):
    return (dx - 1) * 2 * ZN % FAR


GROUPS = [(0, 1)] + [(2 * t - 1, 2) for t in range(1, ZN // 2)] + [(ZN - 1, 1)]
RANGE_AT = sorted(range(ZN), key=place)


def kernel(kb, kc, q_hbm, o_hbm, k_hbm, v_hbm, att_hbm, gq_hbm, outk_ref, outv_ref,
           q_in, o_in, att_s, gq_s, near_k, near_v, stage, other, beyond, terms, terms_far, other_terms, other_sum, other_in, ring, rowsum,
           parts_k, parts_v, own_k, own_v, k_s, v_s, kt_s, vt_s, q_st, o_st, e_s, p_s, ds_s, dp_s, inv_s,
           which_s, slot_s, other_s, load_s, send_sem, recv_sem, local_sem):
    position = lax.axis_index("ctx")
    x = lax.rem(position, XN)
    z = lax.div(position, XN)
    near = [near_k, near_v]
    kv_hbm = [k_hbm, v_hbm]

    def along_x(dx):
        return z * XN + lax.rem(x + dx % XN, XN)

    def along_z(dz):
        return lax.rem(z + dz % ZN, ZN) * XN + x

    barrier = pltpu.get_barrier_semaphore()
    partners = [along_x(d) for d in range(1, XN)] + [along_z(u) for u in range(1, ZN)]
    for partner in partners:
        pl.semaphore_signal(barrier, inc=1, device_id={"ctx": partner}, device_id_type=MESH)

    loads = []
    for i, (src, dst) in enumerate((
            (k_hbm, near_k.at[pl.ds(FAR, BLK_DEV)]), (v_hbm, near_v.at[pl.ds(FAR, BLK_DEV)]),
            (q_hbm, q_in), (o_hbm, o_in))):
        copy = pltpu.make_async_copy(src, dst, local_sem.at[i])
        copy.start()
        loads.append(copy)

    for dx in range(XN):
        reader = along_x(dx) * BLK_DEV
        blocks, owners = [], []
        for e in range(ENTRIES):
            block = kb[e % KSLOTS, reader + e // KSLOTS]
            live = e % KSLOTS < kc[reader + e // KSLOTS]
            blocks.append(lax.rem(block, BLK_DEV))
            owners.append(jnp.where(live, lax.div(block, BLK_DEV), -1))
        for u in range(ZN):
            wanted = along_z(u)
            which = jnp.int32(0)
            for e in range(ENTRIES):
                which = jnp.where(owners[e] == wanted, blocks[e], which)
            which_s[dx * ZN + u] = which
        if dx == 0:
            for ax in range(XN):
                for u in range(ZN):
                    wanted = lax.rem(z + u, ZN) * XN + lax.rem(x + ax, XN)
                    slot = jnp.int32(ENTRIES)
                    for e in range(ENTRIES):
                        slot = jnp.where(owners[e] == wanted, e, slot)
                    slot_s[ax * ZN + u] = slot
    for u in range(ZN):
        reader = along_z(u) * BLK_DEV
        which = jnp.int32(0)
        for e in range(ENTRIES):
            block = kb[e % KSLOTS, reader + e // KSLOTS]
            hit = (e % KSLOTS < kc[reader + e // KSLOTS]) & (lax.div(block, BLK_DEV) == along_x(2))
            which = jnp.where(hit, lax.rem(block, BLK_DEV), which)
        other_s[u] = which
    for b in range(BLK_DEV):
        block = position * BLK_DEV + b
        first = None
        for s in range(KSLOTS):
            listed = kb[s, block]
            owner = lax.div(listed, BLK_DEV)
            dx = lax.rem(lax.rem(owner, XN) - x + XN, XN)
            u = lax.rem(lax.div(owner, XN) - z + ZN, ZN)
            spot = jnp.where(u == 0, 0, jnp.where(u <= ZN // 2, 2 * u - 1, 2 * (ZN - u)))
            at = jnp.where(dx == 0, FAR + BLK_DEV * u + lax.rem(listed, BLK_DEV), lax.rem((dx + 2) * 2 * ZN, FAR) + spot)
            first = at if s == 0 else first
            load_s[b * KSLOTS + s] = jnp.where(s < kc[block], at, first)

    used = [0]

    def fresh():
        used[0] += 1
        return used[0] - 1

    def send(src, dst, device, out, at):
        copy = pltpu.make_async_remote_copy(
            src_ref=src, dst_ref=dst, send_sem=send_sem.at[out], recv_sem=recv_sem.at[at],
            device_id={"ctx": device}, device_id_type=MESH)
        copy.start()
        return copy

    def wait_sent(ref, out):
        pltpu.make_async_remote_copy(
            src_ref=ref, dst_ref=ref, send_sem=send_sem.at[out], recv_sem=recv_sem.at[0],
            device_id={"ctx": partners[0]}, device_id_type=MESH).wait_send()

    def wait_come(ref, at):
        pltpu.make_async_remote_copy(
            src_ref=ref, dst_ref=ref, send_sem=send_sem.at[0], recv_sem=recv_sem.at[at],
            device_id={"ctx": partners[0]}, device_id_type=MESH).wait_recv()

    def column(i, u, half=None):
        first = FAR + BLK_DEV * (u % ZN)
        if half is None:
            return near[i].at[pl.ds(first, BLK_DEV)]
        return near[i].at[pl.ds(first + half, 1)]

    def ring_near(i):
        return {(1, d): send(kv_hbm[i], column(i, -d), along_z(d), i, fresh()) for d in (1, -1)}

    def ring_mid(i):
        return {(2, d): send(column(i, -d), column(i, -2 * d), along_z(d), i, fresh()) for d in (1, -1)}

    def ring_far(i):
        out = {(3, d): send(column(i, -2 * d), column(i, -3 * d), along_z(d), i, fresh()) for d in (1, -1)}
        for half, d in enumerate((1, -1)):
            out[4, d] = send(column(i, -2 * d, half), column(i, 4, half), along_z(2 * d), i, fresh())
        return out

    def spread(phase, group, dst_at, at, at_far):
        first, count = group
        rows = pl.ds(0, CUT)
        send(stage.at[phase, pl.ds(base(2) + first, count), rows], dst_at(2, first, count), along_x(2), 8 + phase, at_far)
        for dx in (1, 3):
            send(stage.at[phase, pl.ds(base(dx) + first, count)], dst_at(XN - dx, first, count), along_x(dx), 4 + phase, at)

    def cross(i):
        return send(kv_hbm[i].at[:, pl.ds(CUT, REST)], other.at[i], along_x(2), 16 + i, fresh())

    def cross_on(i):
        crossing[i].wait_recv()
        rows = pl.ds(CUT, REST)
        low, high = other[i, 0], other[i, 1]
        for u in range(1, ZN):
            beyond[i, u] = jnp.where(other_s[u] == 1, high, low)
            send(beyond.at[i, u], near[i].at[base(2) + place(-u % ZN), rows], along_z(u), 12 + i, beyond_come[i])
        near[i][base(2), CUT:] = jnp.where(other_s[0] == 1, high, low)

    def all_come(i):
        wait_come(near[i].at[pl.ds(0, 2 * ZN)], far_come[i])
        wait_come(near[i].at[pl.ds(2 * ZN, ZN), pl.ds(0, CUT)], opposite_come[i])
        wait_come(near[i].at[pl.ds(2 * ZN + 1, ZN - 1), pl.ds(CUT, REST)], beyond_come[i])

    def choose(i, group):
        first, count = group
        for j in range(first, first + count):
            u = RANGE_AT[j]
            low, high = near[i][FAR + BLK_DEV * u], near[i][FAR + BLK_DEV * u + 1]
            for dx in range(1, XN):
                stage[i, base(dx) + j] = jnp.where(which_s[dx * ZN + u] == 1, high, low)

    pl.semaphore_wait(barrier, len(partners))

    top = ZN // 2
    far_come = [fresh(), fresh()]
    opposite_come = [fresh(), fresh()]
    beyond_come = [fresh(), fresh()]
    crossing = [None, None]
    rings = [{}, {}]

    def gather_x(i, t):
        choose(i, GROUPS[t])
        def at(dx, first, count):
            slots = pl.ds(base(dx) + first, count)
            return near[i].at[slots] if dx != 2 else near[i].at[slots, pl.ds(0, CUT)]

        spread(i, GROUPS[t], at, far_come[i], opposite_come[i])

    def come(i, t):
        for d in (1, -1):
            rings[i][t, d].wait_recv()

    rings[0].update(ring_near(0))
    crossing[0] = cross(0)
    loads[0].wait()
    gather_x(0, 0)
    rings[1].update(ring_near(1))
    come(0, 1)
    rings[0].update(ring_mid(0))
    gather_x(0, 1)
    crossing[1] = cross(1)
    cross_on(0)
    loads[1].wait()
    gather_x(1, 0)
    come(1, 1)
    rings[1].update(ring_mid(1))
    come(0, 2)
    rings[0].update(ring_far(0))
    gather_x(0, 2)
    gather_x(1, 1)
    cross_on(1)
    come(1, 2)
    rings[1].update(ring_far(1))
    come(0, 3)
    gather_x(0, 3)
    come(0, 4)
    gather_x(0, 4)
    gather_x(1, 2)
    come(1, 3)
    gather_x(1, 3)
    come(1, 4)
    gather_x(1, 4)
    loads[2].wait()
    loads[3].wait()
    all_come(0)

    def rows_of(s):
        return pl.ds(s * BLOCK, BLOCK)

    def fetch(i, b):
        full, turned = (k_s, kt_s) if i == 0 else (v_s, vt_s)
        for s in range(NSLOT):
            at = FAR + b if s == 0 else load_s[b * KSLOTS + s - 1]
            block = near[i][at]
            full[b, rows_of(s), :] = block
            turned[b, :, rows_of(s)] = block.T

    def bias(b, s):
        return jnp.where(s < kc[position * BLK_DEV + b], 0.0, NEG).astype(F32)

    def probs(b, pair):
        cols = pl.ds(pair * 2 * BLOCK, 2 * BLOCK)
        for h in (2 * pair, 2 * pair + 1):
            q_st[b, pl.ds(h * BLOCK, BLOCK), :] = q_in[b, :, pl.ds(h * DH, DH)]
            o_st[b, pl.ds(h * BLOCK, BLOCK), :] = o_in[b, :, pl.ds(h * DH, DH)]
        q2 = q_st[b, cols, :]
        m = None
        e_s[b, :, cols] = lax.dot_general(k_s[b], q2, NT, preferred_element_type=F32)
        for s in range(NSLOT):
            high = jnp.max(e_s[b, rows_of(s), cols], axis=0, keepdims=True)
            if s > 0:
                high = high + bias(b, s - 1)
            m = high if m is None else jnp.maximum(m, high)
        mc = m * SCALE2
        total = None
        for s in range(NSLOT):
            off = -mc if s == 0 else bias(b, s - 1) - mc
            e = jnp.exp2(e_s[b, rows_of(s), cols] * SCALE2 + off)
            e_s[b, rows_of(s), cols] = e
            part = jnp.sum(e, axis=0, keepdims=True)
            total = part if total is None else total + part
        inv = 1.0 / total
        inv_s[b, :, cols] = jnp.broadcast_to(inv, (8, 2 * BLOCK))
        for s in range(NSLOT):
            p_s[b, rows_of(s), cols] = (e_s[b, rows_of(s), cols] * inv).astype(BF16)

    def key_side(b, weights, rows_in, parts, own):
        g = jnp.dot(weights[b], rows_in[b], preferred_element_type=F32)
        own[b] = g[:BLOCK]
        for s in range(KSLOTS):
            parts[b * KSLOTS + s] = g[(s + 1) * BLOCK:(s + 2) * BLOCK].astype(BF16)

    def query_side(b, pair):
        cols = pl.ds(pair * 2 * BLOCK, 2 * BLOCK)
        o2 = o_st[b, cols, :]
        dp_s[...] = lax.dot_general(v_s[b], o2, NT, preferred_element_type=F32)
        out_t = jnp.dot(vt_s[b], p_s[b, :, cols], preferred_element_type=F32)
        att_t = out_t.astype(BF16)
        delta = jnp.sum(o2.T.astype(F32) * att_t.astype(F32), axis=0, keepdims=True)
        inv = inv_s[b, pl.ds(0, 1), cols] * SCALING
        for s in range(NSLOT):
            dp = dp_s[rows_of(s), :]
            ds_s[b, rows_of(s), cols] = ((e_s[b, rows_of(s), cols] * inv) * (dp - delta)).astype(BF16)
        gq_t = jnp.dot(kt_s[b], ds_s[b, :, cols], preferred_element_type=F32).astype(BF16)
        att, gq = att_t.T, gq_t.T
        for j in (0, 1):
            h = pl.ds((2 * pair + j) * DH, DH)
            att_s[b, :, h] = att[j * BLOCK:(j + 1) * BLOCK]
            gq_s[b, :, h] = gq[j * BLOCK:(j + 1) * BLOCK]

    parts = [parts_k, parts_v]

    terms_come = {}

    def scatter_x(i, t):
        first, count = GROUPS[t]
        for j in range(first, first + count):
            for dx in range(1, XN):
                stage[2 + i, base(dx) + j] = parts[i][slot_s[dx * ZN + RANGE_AT[j]]]
        terms_come[i, t] = fresh(), fresh()

        def at(dx, first, count):
            return terms.at[i, pl.ds(first, count), dx // 2] if dx != 2 else terms_far.at[i, pl.ds(first, count)]

        spread(2 + i, GROUPS[t], at, *terms_come[i, t])

    def scatter_cross(i):
        terms_come[i] = fresh()
        for u in range(1, ZN):
            beyond[2 + i, u] = parts[i][slot_s[2 * ZN + u], pl.ds(CUT, REST)]
            send(beyond.at[2 + i, u], other_terms.at[i, -u % ZN], along_z(u), 14 + i, terms_come[i])

    def cross_sums(i):
        wait_come(other_terms.at[i, pl.ds(1, ZN - 1)], terms_come[i])
        low = high = None
        for u in range(ZN):
            term = (parts[i][slot_s[2 * ZN], pl.ds(CUT, REST)] if u == 0 else other_terms[i, u]).astype(F32)
            second = other_s[u] == 1
            up = jnp.where(second, term, 0.0)
            down = jnp.where(second, 0.0, term)
            high = up if high is None else high + up
            low = down if low is None else low + down
        other_sum[i, 0] = low.astype(BF16)
        other_sum[i, 1] = high.astype(BF16)
        crossing[i] = send(other_sum.at[i], other_in.at[i], along_x(2), 18 + i, fresh())

    def row_sums(i, t):
        first, count = GROUPS[t]
        wait_come(terms.at[i, pl.ds(first, count)], terms_come[i, t][0])
        wait_come(terms_far.at[i, pl.ds(first, count)], terms_come[i, t][1])
        for j in range(first, first + count):
            u = RANGE_AT[j]
            for start, size in ((0, CUT), (CUT, REST)):
                rows = pl.ds(start, size)
                low = high = None
                for dx in range(XN):
                    if dx == 0 and u == 0 or dx == 2 and start > 0:
                        continue
                    if dx == 0:
                        term = parts[i][slot_s[u], rows]
                    else:
                        term = terms_far[i, j] if dx == 2 else terms[i, j, dx // 2, rows]
                    term = term.astype(F32)
                    second = which_s[dx * ZN + u] == 1
                    up = jnp.where(second, term, 0.0)
                    down = jnp.where(second, 0.0, term)
                    high = up if high is None else high + up
                    low = down if low is None else low + down
                rowsum[i, u, 0, rows] = low.astype(BF16)
                rowsum[i, u, 1, rows] = high.astype(BF16)

    chains = [{}, {}]

    def chain(i, t):
        for j, d in enumerate((1, -1)):
            u = (-d * t) % ZN
            dst = ring.at[i, j, t - 1]
            src = rowsum.at[i, u]
            if t == 4:
                src, dst = src.at[pl.ds(j, 1)], dst.at[pl.ds(j, 1)]
            if t == 2:
                chains[i][3, d].wait_recv()
                chains[i][4, d].wait_recv()
                for w in range(BLK_DEV):
                    both = rowsum[i, u, w].astype(F32) + ring[i, j, 2, w].astype(F32)
                    if w == j:
                        both = both + ring[i, j, 3, w].astype(F32)
                    rowsum[i, u, w] = both.astype(BF16)
            chains[i][t, d] = send(src, dst, along_z(-d * t if t < 3 else (2 - t) * d), 2 + i, fresh())

    def finish(i):
        for t in (1, 2):
            for d in (1, -1):
                chains[i][t, d].wait_recv()
        crossing[i].wait_recv()
        own = (own_k, own_v)[i]
        out = (outk_ref, outv_ref)[i]
        for w in range(BLK_DEV):
            total = own[w] + rowsum[i, 0, w].astype(F32)
            for t in (1, 2):
                for j in (0, 1):
                    total = total + ring[i, j, t - 1, w].astype(F32)
            out[w, :CUT] = total[:CUT].astype(BF16)
            out[w, CUT:] = (total[CUT:] + other_in[i, w].astype(F32)).astype(BF16)

    pairs = GROUP // 2
    units = [(b, pair) for b in range(BLK_DEV) for pair in range(pairs)]
    for i in (0, 1):
        parts[i][ENTRIES] = jnp.zeros((BLOCK, DH), BF16)
    for b, pair in units:
        if pair == 0:
            fetch(0, b)
        probs(b, pair)
        if pair == pairs - 1:
            key_side(b, p_s, o_st, parts_v, own_v)
    scatter_cross(1)
    for t in range(top, -1, -1):
        scatter_x(1, t)
    all_come(1)
    stores = []

    def sums_on(i, t):
        row_sums(i, t)
        if t in (4, 3, 1):
            chain(i, t)
        if t == 1:
            chain(i, 2)

    for n, (b, pair) in enumerate(units):
        if pair == 0:
            fetch(1, b)
        query_side(b, pair)
        if n == 5:
            sums_on(1, 4)
        if n == 7:
            sums_on(1, 3)
        if pair == pairs - 1:
            key_side(b, ds_s, q_st, parts_k, own_k)
            for src, dst in ((att_s, att_hbm), (gq_s, gq_hbm)):
                copy = pltpu.make_async_copy(src.at[b], dst.at[b], local_sem.at[4 + len(stores)])
                copy.start()
                stores.append(copy)
    scatter_cross(0)
    for t in range(top, -1, -1):
        scatter_x(0, t)
    cross_sums(1)
    for t in (2, 1, 0):
        sums_on(1, t)
    for t in range(top, -1, -1):
        sums_on(0, t)
        if t == 3:
            cross_sums(0)
    finish(1)
    finish(0)
    for i in (0, 1):
        ring_bytes = near[i].at[pl.ds(0, 7 * BLK_DEV)]
        wait_sent(ring_bytes, i)
        wait_sent(ring_bytes, 2 + i)
    for phase in range(4):
        wait_sent(stage.at[phase, pl.ds(0, 2 * ZN)], 4 + phase)
        wait_sent(stage.at[phase, pl.ds(2 * ZN, ZN), pl.ds(0, CUT)], 8 + phase)
        wait_sent(beyond.at[phase, pl.ds(1, ZN - 1)], 12 + phase)
    for i in (0, 1):
        wait_sent(other.at[i], 16 + i)
        wait_sent(other_sum.at[i], 18 + i)
    for copy in stores:
        copy.wait()


def hand_on(*refs):
    inputs, outputs, held, sems = refs[:4], refs[4:8], refs[8:12], refs[12]
    parts = [(i, pl.ds(p * BLOCK, BLOCK)) for i in range(4) for p in range(BLK_DEV)]
    reads = [pltpu.make_async_copy(inputs[i].at[rows], held[i].at[rows], sems.at[0, n]) for n, (i, rows) in enumerate(parts)]
    writes = [pltpu.make_async_copy(held[i].at[rows], outputs[i].at[rows], sems.at[1, n]) for n, (i, rows) in enumerate(parts)]
    for copy in reads:
        copy.start()
    for read, write in zip(reads, writes):
        read.wait()
        write.start()
    for copy in writes:
        copy.wait()


def local(queries, keys, values, grad_out, key_blocks, key_count):
    rows, width = queries.shape
    wide = (BLK_DEV, BLOCK, width)
    own = (BLK_DEV, BLOCK, DH)
    any_spec = pl.BlockSpec(memory_space=pl.ANY)
    smem_spec = pl.BlockSpec(memory_space=pltpu.SMEM)
    vmem_spec = pl.BlockSpec(memory_space=pltpu.VMEM)
    vmem = pltpu.VMEM
    att, gq, gk, gv = pl.pallas_call(
        kernel,
        out_shape=[jax.ShapeDtypeStruct(wide, BF16)] * 2 + [jax.ShapeDtypeStruct(own, BF16)] * 2,
        in_specs=[smem_spec] * 2 + [any_spec] * 4,
        out_specs=[any_spec] * 2 + [vmem_spec] * 2,
        scratch_shapes=[
            vmem(wide, BF16), vmem(wide, BF16), vmem(wide, BF16), vmem(wide, BF16),
            vmem((FAR + BLK_DEV * ZN, BLOCK, DH), BF16), vmem((FAR + BLK_DEV * ZN, BLOCK, DH), BF16),
            vmem((4, FAR, BLOCK, DH), BF16), vmem((2, BLK_DEV, REST, DH), BF16), vmem((4, ZN, REST, DH), BF16),
            vmem((2, ZN, 2, BLOCK, DH), BF16), vmem((2, ZN, CUT, DH), BF16),
            vmem((2, ZN, REST, DH), BF16), vmem((2, BLK_DEV, REST, DH), BF16), vmem((2, BLK_DEV, REST, DH), BF16),

            vmem((2, 2, ZN // 2, BLK_DEV, BLOCK, DH), BF16), vmem((2, ZN, BLK_DEV, BLOCK, DH), BF16),
            vmem((ENTRIES + 1, BLOCK, DH), BF16), vmem((ENTRIES + 1, BLOCK, DH), BF16),
            vmem(own, F32), vmem(own, F32),
            vmem((BLK_DEV, WIDE, DH), BF16), vmem((BLK_DEV, WIDE, DH), BF16),
            vmem((BLK_DEV, DH, WIDE), BF16), vmem((BLK_DEV, DH, WIDE), BF16),
            vmem((BLK_DEV, GROUP * BLOCK, DH), BF16), vmem((BLK_DEV, GROUP * BLOCK, DH), BF16),
            vmem((BLK_DEV, WIDE, GROUP * BLOCK), F32),
            vmem((BLK_DEV, WIDE, GROUP * BLOCK), BF16), vmem((BLK_DEV, WIDE, GROUP * BLOCK), BF16),
            vmem((WIDE, 2 * BLOCK), F32), vmem((BLK_DEV, 8, GROUP * BLOCK), F32),
            pltpu.SMEM((XN * ZN,), jnp.int32), pltpu.SMEM((XN * ZN,), jnp.int32), pltpu.SMEM((ZN,), jnp.int32), pltpu.SMEM((ENTRIES,), jnp.int32),
            pltpu.SemaphoreType.DMA((SENDS,)), pltpu.SemaphoreType.DMA((RECVS,)), pltpu.SemaphoreType.DMA((8,))],
        compiler_params=pltpu.CompilerParams(collective_id=0, has_side_effects=True, vmem_limit_bytes=56 << 20),
        name="sparse_attention",
    )(key_blocks.T, key_count, queries.reshape(wide), grad_out.reshape(wide), keys.reshape(own), values.reshape(own))
    results = [att.reshape(rows, width), gq.reshape(rows, width), gk.reshape(rows, DH), gv.reshape(rows, DH)]
    return tuple(pl.pallas_call(
        hand_on,
        out_shape=[jax.ShapeDtypeStruct(a.shape, a.dtype) for a in results],
        in_specs=[any_spec] * 4,
        out_specs=[any_spec] * 4,
        scratch_shapes=[vmem(a.shape, a.dtype) for a in results] + [pltpu.SemaphoreType.DMA((2, 4 * BLK_DEV))],
        name="hand_on",
    )(*results))


def solution(mesh):
    in_specs = (P("ctx", "head"), P("ctx", "head"), P("ctx", "head"), P("ctx", "head"), P(), P())
    out_specs = (P("ctx", "head"), P("ctx", "head"), P("ctx", "head"), P("ctx", "head"))
    return jax.shard_map(local, mesh=mesh, in_specs=in_specs, out_specs=out_specs, check_vma=False)
```

```python
import functools
import math

import jax
import jax.numpy as jnp
from jax import lax
from jax.experimental import pallas as pl
from jax.experimental.pallas import tpu as pltpu
from jax.sharding import PartitionSpec as P

QH = 64
KVH = 8
DH = 128
BLOCK = 128
KSLOTS = 6
NSLOT = KSLOTS + 1
GROUP = QH // KVH
BLK_DEV = 2
ENTRIES = BLK_DEV * KSLOTS
XN = 4
ZN = 8
FAR = (XN - 1) * ZN
WIDE = NSLOT * BLOCK
SCALING = 1.0 / math.sqrt(DH)
SCALE2 = SCALING * 1.4426950408889634
NEG = -1e30
SENDS = 20
RECVS = 64
CUT = 80
REST = BLOCK - CUT
MESH = pl.DeviceIdType.MESH
BF16 = jnp.bfloat16
F32 = jnp.float32
NT = (((1,), (1,)), ((), ()))


def place(u):
    return 0 if u == 0 else (2 * u - 1 if u <= ZN // 2 else 2 * (ZN - u))


def base(dx):
    return (dx - 1) * 2 * ZN % FAR


GROUPS = [(0, 1)] + [(2 * t - 1, 2) for t in range(1, ZN // 2)] + [(ZN - 1, 1)]
RANGE_AT = sorted(range(ZN), key=place)


def kernel(kb, kc, q_hbm, o_hbm, k_hbm, v_hbm, att_hbm, gq_hbm, outk_ref, outv_ref,
           q_in, o_in, att_s, gq_s, near_k, near_v, stage, other, beyond, terms, terms_far, other_terms, other_sum, other_in, ring, rowsum,
           parts_k, parts_v, own_k, own_v, k_s, v_s, kt_s, vt_s, q_st, o_st, e_s, p_s, ds_s, dp_s, inv_s,
           which_s, slot_s, other_s, load_s, send_sem, recv_sem, local_sem):
    position = lax.axis_index("ctx")
    x = lax.rem(position, XN)
    z = lax.div(position, XN)
    near = [near_k, near_v]
    kv_hbm = [k_hbm, v_hbm]

    def along_x(dx):
        return z * XN + lax.rem(x + dx % XN, XN)

    def along_z(dz):
        return lax.rem(z + dz % ZN, ZN) * XN + x

    barrier = pltpu.get_barrier_semaphore()
    partners = [along_x(d) for d in range(1, XN)] + [along_z(u) for u in range(1, ZN)]
    for partner in partners:
        pl.semaphore_signal(barrier, inc=1, device_id={"ctx": partner}, device_id_type=MESH)

    loads = []
    for i, (src, dst) in enumerate((
            (k_hbm, near_k.at[pl.ds(FAR, BLK_DEV)]), (v_hbm, near_v.at[pl.ds(FAR, BLK_DEV)]),
            (q_hbm, q_in), (o_hbm, o_in))):
        copy = pltpu.make_async_copy(src, dst, local_sem.at[i])
        copy.start()
        loads.append(copy)

    for dx in range(XN):
        reader = along_x(dx) * BLK_DEV
        blocks, owners = [], []
        for e in range(ENTRIES):
            block = kb[e % KSLOTS, reader + e // KSLOTS]
            live = e % KSLOTS < kc[reader + e // KSLOTS]
            blocks.append(lax.rem(block, BLK_DEV))
            owners.append(jnp.where(live, lax.div(block, BLK_DEV), -1))
        for u in range(ZN):
            wanted = along_z(u)
            which = jnp.int32(0)
            for e in range(ENTRIES):
                which = jnp.where(owners[e] == wanted, blocks[e], which)
            which_s[dx * ZN + u] = which
        if dx == 0:
            for ax in range(XN):
                for u in range(ZN):
                    wanted = lax.rem(z + u, ZN) * XN + lax.rem(x + ax, XN)
                    slot = jnp.int32(ENTRIES)
                    for e in range(ENTRIES):
                        slot = jnp.where(owners[e] == wanted, e, slot)
                    slot_s[ax * ZN + u] = slot
    for u in range(ZN):
        reader = along_z(u) * BLK_DEV
        which = jnp.int32(0)
        for e in range(ENTRIES):
            block = kb[e % KSLOTS, reader + e // KSLOTS]
            hit = (e % KSLOTS < kc[reader + e // KSLOTS]) & (lax.div(block, BLK_DEV) == along_x(2))
            which = jnp.where(hit, lax.rem(block, BLK_DEV), which)
        other_s[u] = which
    for b in range(BLK_DEV):
        block = position * BLK_DEV + b
        first = None
        for s in range(KSLOTS):
            listed = kb[s, block]
            owner = lax.div(listed, BLK_DEV)
            dx = lax.rem(lax.rem(owner, XN) - x + XN, XN)
            u = lax.rem(lax.div(owner, XN) - z + ZN, ZN)
            spot = jnp.where(u == 0, 0, jnp.where(u <= ZN // 2, 2 * u - 1, 2 * (ZN - u)))
            at = jnp.where(dx == 0, FAR + BLK_DEV * u + lax.rem(listed, BLK_DEV), lax.rem((dx + 2) * 2 * ZN, FAR) + spot)
            first = at if s == 0 else first
            load_s[b * KSLOTS + s] = jnp.where(s < kc[block], at, first)

    used = [0]

    def fresh():
        used[0] += 1
        return used[0] - 1

    def send(src, dst, device, out, at):
        copy = pltpu.make_async_remote_copy(
            src_ref=src, dst_ref=dst, send_sem=send_sem.at[out], recv_sem=recv_sem.at[at],
            device_id={"ctx": device}, device_id_type=MESH)
        copy.start()
        return copy

    def wait_sent(ref, out):
        pltpu.make_async_remote_copy(
            src_ref=ref, dst_ref=ref, send_sem=send_sem.at[out], recv_sem=recv_sem.at[0],
            device_id={"ctx": partners[0]}, device_id_type=MESH).wait_send()

    def wait_come(ref, at):
        pltpu.make_async_remote_copy(
            src_ref=ref, dst_ref=ref, send_sem=send_sem.at[0], recv_sem=recv_sem.at[at],
            device_id={"ctx": partners[0]}, device_id_type=MESH).wait_recv()

    def column(i, u, half=None):
        first = FAR + BLK_DEV * (u % ZN)
        if half is None:
            return near[i].at[pl.ds(first, BLK_DEV)]
        return near[i].at[pl.ds(first + half, 1)]

    def ring_near(i):
        return {(1, d): send(kv_hbm[i], column(i, -d), along_z(d), i, fresh()) for d in (1, -1)}

    def ring_mid(i):
        return {(2, d): send(column(i, -d), column(i, -2 * d), along_z(d), i, fresh()) for d in (1, -1)}

    def ring_far(i):
        out = {(3, d): send(column(i, -2 * d), column(i, -3 * d), along_z(d), i, fresh()) for d in (1, -1)}
        for half, d in enumerate((1, -1)):
            out[4, d] = send(column(i, -2 * d, half), column(i, 4, half), along_z(2 * d), i, fresh())
        return out

    def spread(phase, group, dst_at, at, at_far):
        first, count = group
        rows = pl.ds(0, CUT)
        send(stage.at[phase, pl.ds(base(2) + first, count), rows], dst_at(2, first, count), along_x(2), 8 + phase, at_far)
        for dx in (1, 3):
            send(stage.at[phase, pl.ds(base(dx) + first, count)], dst_at(XN - dx, first, count), along_x(dx), 4 + phase, at)

    def cross(i):
        return send(kv_hbm[i].at[:, pl.ds(CUT, REST)], other.at[i], along_x(2), 16 + i, fresh())

    def cross_on(i):
        crossing[i].wait_recv()
        rows = pl.ds(CUT, REST)
        low, high = other[i, 0], other[i, 1]
        for u in range(1, ZN):
            beyond[i, u] = jnp.where(other_s[u] == 1, high, low)
            send(beyond.at[i, u], near[i].at[base(2) + place(-u % ZN), rows], along_z(u), 12 + i, beyond_come[i])
        near[i][base(2), CUT:] = jnp.where(other_s[0] == 1, high, low)

    def all_come(i):
        wait_come(near[i].at[pl.ds(0, 2 * ZN)], far_come[i])
        wait_come(near[i].at[pl.ds(2 * ZN, ZN), pl.ds(0, CUT)], opposite_come[i])
        wait_come(near[i].at[pl.ds(2 * ZN + 1, ZN - 1), pl.ds(CUT, REST)], beyond_come[i])

    def choose(i, group):
        first, count = group
        for j in range(first, first + count):
            u = RANGE_AT[j]
            low, high = near[i][FAR + BLK_DEV * u], near[i][FAR + BLK_DEV * u + 1]
            for dx in range(1, XN):
                stage[i, base(dx) + j] = jnp.where(which_s[dx * ZN + u] == 1, high, low)

    pl.semaphore_wait(barrier, len(partners))

    top = ZN // 2
    far_come = [fresh(), fresh()]
    opposite_come = [fresh(), fresh()]
    beyond_come = [fresh(), fresh()]
    crossing = [None, None]
    rings = [{}, {}]

    def gather_x(i, t):
        choose(i, GROUPS[t])
        def at(dx, first, count):
            slots = pl.ds(base(dx) + first, count)
            return near[i].at[slots] if dx != 2 else near[i].at[slots, pl.ds(0, CUT)]

        spread(i, GROUPS[t], at, far_come[i], opposite_come[i])

    def come(i, t):
        for d in (1, -1):
            rings[i][t, d].wait_recv()

    rings[0].update(ring_near(0))
    rings[1].update(ring_near(1))
    crossing[0] = cross(0)
    crossing[1] = cross(1)
    loads[0].wait()
    gather_x(0, 0)
    loads[1].wait()
    gather_x(1, 0)
    come(0, 1)
    rings[0].update(ring_mid(0))
    gather_x(0, 1)
    come(1, 1)
    rings[1].update(ring_mid(1))
    gather_x(1, 1)
    cross_on(0)
    come(0, 2)
    rings[0].update(ring_far(0))
    gather_x(0, 2)
    cross_on(1)
    come(1, 2)
    rings[1].update(ring_far(1))
    gather_x(1, 2)
    come(0, 3)
    gather_x(0, 3)
    come(0, 4)
    gather_x(0, 4)
    come(1, 3)
    gather_x(1, 3)
    come(1, 4)
    gather_x(1, 4)
    loads[2].wait()
    loads[3].wait()
    all_come(0)

    def rows_of(s):
        return pl.ds(s * BLOCK, BLOCK)

    def fetch(i, b):
        full, turned = (k_s, kt_s) if i == 0 else (v_s, vt_s)
        for s in range(NSLOT):
            at = FAR + b if s == 0 else load_s[b * KSLOTS + s - 1]
            block = near[i][at]
            full[b, rows_of(s), :] = block
            turned[b, :, rows_of(s)] = block.T

    def bias(b, s):
        return jnp.where(s < kc[position * BLK_DEV + b], 0.0, NEG).astype(F32)

    def probs(b, pair):
        cols = pl.ds(pair * 2 * BLOCK, 2 * BLOCK)
        for h in (2 * pair, 2 * pair + 1):
            q_st[b, pl.ds(h * BLOCK, BLOCK), :] = q_in[b, :, pl.ds(h * DH, DH)]
            o_st[b, pl.ds(h * BLOCK, BLOCK), :] = o_in[b, :, pl.ds(h * DH, DH)]
        q2 = q_st[b, cols, :]
        m = None
        e_s[b, :, cols] = lax.dot_general(k_s[b], q2, NT, preferred_element_type=F32)
        for s in range(NSLOT):
            high = jnp.max(e_s[b, rows_of(s), cols], axis=0, keepdims=True)
            if s > 0:
                high = high + bias(b, s - 1)
            m = high if m is None else jnp.maximum(m, high)
        mc = m * SCALE2
        total = None
        for s in range(NSLOT):
            off = -mc if s == 0 else bias(b, s - 1) - mc
            e = jnp.exp2(e_s[b, rows_of(s), cols] * SCALE2 + off)
            e_s[b, rows_of(s), cols] = e
            part = jnp.sum(e, axis=0, keepdims=True)
            total = part if total is None else total + part
        inv = 1.0 / total
        inv_s[b, :, cols] = jnp.broadcast_to(inv, (8, 2 * BLOCK))
        for s in range(NSLOT):
            p_s[b, rows_of(s), cols] = (e_s[b, rows_of(s), cols] * inv).astype(BF16)

    def key_side(b, weights, rows_in, parts, own):
        g = jnp.dot(weights[b], rows_in[b], preferred_element_type=F32)
        own[b] = g[:BLOCK]
        for s in range(KSLOTS):
            parts[b * KSLOTS + s] = g[(s + 1) * BLOCK:(s + 2) * BLOCK].astype(BF16)

    def query_side(b, pair):
        cols = pl.ds(pair * 2 * BLOCK, 2 * BLOCK)
        o2 = o_st[b, cols, :]
        dp_s[...] = lax.dot_general(v_s[b], o2, NT, preferred_element_type=F32)
        out_t = jnp.dot(vt_s[b], p_s[b, :, cols], preferred_element_type=F32)
        att_t = out_t.astype(BF16)
        delta = jnp.sum(o2.T.astype(F32) * att_t.astype(F32), axis=0, keepdims=True)
        inv = inv_s[b, pl.ds(0, 1), cols] * SCALING
        for s in range(NSLOT):
            dp = dp_s[rows_of(s), :]
            ds_s[b, rows_of(s), cols] = ((e_s[b, rows_of(s), cols] * inv) * (dp - delta)).astype(BF16)
        gq_t = jnp.dot(kt_s[b], ds_s[b, :, cols], preferred_element_type=F32).astype(BF16)
        att, gq = att_t.T, gq_t.T
        for j in (0, 1):
            h = pl.ds((2 * pair + j) * DH, DH)
            att_s[b, :, h] = att[j * BLOCK:(j + 1) * BLOCK]
            gq_s[b, :, h] = gq[j * BLOCK:(j + 1) * BLOCK]

    parts = [parts_k, parts_v]

    terms_come = {}

    def scatter_x(i, t):
        first, count = GROUPS[t]
        for j in range(first, first + count):
            for dx in range(1, XN):
                stage[2 + i, base(dx) + j] = parts[i][slot_s[dx * ZN + RANGE_AT[j]]]
        terms_come[i, t] = fresh(), fresh()

        def at(dx, first, count):
            return terms.at[i, pl.ds(first, count), dx // 2] if dx != 2 else terms_far.at[i, pl.ds(first, count)]

        spread(2 + i, GROUPS[t], at, *terms_come[i, t])

    def scatter_cross(i):
        terms_come[i] = fresh()
        for u in range(1, ZN):
            beyond[2 + i, u] = parts[i][slot_s[2 * ZN + u], pl.ds(CUT, REST)]
            send(beyond.at[2 + i, u], other_terms.at[i, -u % ZN], along_z(u), 14 + i, terms_come[i])

    def cross_sums(i):
        wait_come(other_terms.at[i, pl.ds(1, ZN - 1)], terms_come[i])
        low = high = None
        for u in range(ZN):
            term = (parts[i][slot_s[2 * ZN], pl.ds(CUT, REST)] if u == 0 else other_terms[i, u]).astype(F32)
            second = other_s[u] == 1
            up = jnp.where(second, term, 0.0)
            down = jnp.where(second, 0.0, term)
            high = up if high is None else high + up
            low = down if low is None else low + down
        other_sum[i, 0] = low.astype(BF16)
        other_sum[i, 1] = high.astype(BF16)
        crossing[i] = send(other_sum.at[i], other_in.at[i], along_x(2), 18 + i, fresh())

    def row_sums(i, t):
        first, count = GROUPS[t]
        wait_come(terms.at[i, pl.ds(first, count)], terms_come[i, t][0])
        wait_come(terms_far.at[i, pl.ds(first, count)], terms_come[i, t][1])
        for j in range(first, first + count):
            u = RANGE_AT[j]
            for start, size in ((0, CUT), (CUT, REST)):
                rows = pl.ds(start, size)
                low = high = None
                for dx in range(XN):
                    if dx == 0 and u == 0 or dx == 2 and start > 0:
                        continue
                    if dx == 0:
                        term = parts[i][slot_s[u], rows]
                    else:
                        term = terms_far[i, j] if dx == 2 else terms[i, j, dx // 2, rows]
                    term = term.astype(F32)
                    second = which_s[dx * ZN + u] == 1
                    up = jnp.where(second, term, 0.0)
                    down = jnp.where(second, 0.0, term)
                    high = up if high is None else high + up
                    low = down if low is None else low + down
                rowsum[i, u, 0, rows] = low.astype(BF16)
                rowsum[i, u, 1, rows] = high.astype(BF16)

    chains = [{}, {}]

    def chain(i, t):
        for j, d in enumerate((1, -1)):
            u = (-d * t) % ZN
            dst = ring.at[i, j, t - 1]
            src = rowsum.at[i, u]
            if t == 4:
                src, dst = src.at[pl.ds(j, 1)], dst.at[pl.ds(j, 1)]
            if t == 2:
                chains[i][3, d].wait_recv()
                chains[i][4, d].wait_recv()
                for w in range(BLK_DEV):
                    both = rowsum[i, u, w].astype(F32) + ring[i, j, 2, w].astype(F32)
                    if w == j:
                        both = both + ring[i, j, 3, w].astype(F32)
                    rowsum[i, u, w] = both.astype(BF16)
            chains[i][t, d] = send(src, dst, along_z(-d * t if t < 3 else (2 - t) * d), 2 + i, fresh())

    def finish(i):
        for t in (1, 2):
            for d in (1, -1):
                chains[i][t, d].wait_recv()
        crossing[i].wait_recv()
        own = (own_k, own_v)[i]
        out = (outk_ref, outv_ref)[i]
        for w in range(BLK_DEV):
            total = own[w] + rowsum[i, 0, w].astype(F32)
            for t in (1, 2):
                for j in (0, 1):
                    total = total + ring[i, j, t - 1, w].astype(F32)
            out[w, :CUT] = total[:CUT].astype(BF16)
            out[w, CUT:] = (total[CUT:] + other_in[i, w].astype(F32)).astype(BF16)

    pairs = GROUP // 2
    units = [(b, pair) for b in range(BLK_DEV) for pair in range(pairs)]
    for i in (0, 1):
        parts[i][ENTRIES] = jnp.zeros((BLOCK, DH), BF16)
    for b, pair in units:
        if pair == 0:
            fetch(0, b)
        probs(b, pair)
        if pair == pairs - 1:
            key_side(b, p_s, o_st, parts_v, own_v)
    for t in range(top, -1, -1):
        scatter_x(1, t)
    scatter_cross(1)
    all_come(1)
    stores = []

    def sums_on(i, t):
        row_sums(i, t)
        if t in (4, 3, 1):
            chain(i, t)
        if t == 1:
            chain(i, 2)

    for n, (b, pair) in enumerate(units):
        if pair == 0:
            fetch(1, b)
        query_side(b, pair)
        if n == 5:
            sums_on(1, 4)
        if n == 7:
            sums_on(1, 3)
        if pair == pairs - 1:
            key_side(b, ds_s, q_st, parts_k, own_k)
            for src, dst in ((att_s, att_hbm), (gq_s, gq_hbm)):
                copy = pltpu.make_async_copy(src.at[b], dst.at[b], local_sem.at[4 + len(stores)])
                copy.start()
                stores.append(copy)
    scatter_x(0, 4)
    scatter_x(0, 3)
    scatter_cross(0)
    for t in (2, 1, 0):
        scatter_x(0, t)
    cross_sums(1)
    for t in (2, 1, 0):
        sums_on(1, t)
    for t in range(top, -1, -1):
        sums_on(0, t)
        if t == 3:
            cross_sums(0)
    finish(1)
    finish(0)
    for i in (0, 1):
        ring_bytes = near[i].at[pl.ds(0, 7 * BLK_DEV)]
        wait_sent(ring_bytes, i)
        wait_sent(ring_bytes, 2 + i)
    for phase in range(4):
        wait_sent(stage.at[phase, pl.ds(0, 2 * ZN)], 4 + phase)
        wait_sent(stage.at[phase, pl.ds(2 * ZN, ZN), pl.ds(0, CUT)], 8 + phase)
        wait_sent(beyond.at[phase, pl.ds(1, ZN - 1)], 12 + phase)
    for i in (0, 1):
        wait_sent(other.at[i], 16 + i)
        wait_sent(other_sum.at[i], 18 + i)
    for copy in stores:
        copy.wait()


def hand_on(*refs):
    inputs, outputs, held, sems = refs[:4], refs[4:8], refs[8:12], refs[12]
    parts = [(i, pl.ds(p * BLOCK, BLOCK)) for i in range(4) for p in range(BLK_DEV)]
    reads = [pltpu.make_async_copy(inputs[i].at[rows], held[i].at[rows], sems.at[0, n]) for n, (i, rows) in enumerate(parts)]
    writes = [pltpu.make_async_copy(held[i].at[rows], outputs[i].at[rows], sems.at[1, n]) for n, (i, rows) in enumerate(parts)]
    for copy in reads:
        copy.start()
    for read, write in zip(reads, writes):
        read.wait()
        write.start()
    for copy in writes:
        copy.wait()


def local(queries, keys, values, grad_out, key_blocks, key_count):
    rows, width = queries.shape
    wide = (BLK_DEV, BLOCK, width)
    own = (BLK_DEV, BLOCK, DH)
    any_spec = pl.BlockSpec(memory_space=pl.ANY)
    smem_spec = pl.BlockSpec(memory_space=pltpu.SMEM)
    vmem_spec = pl.BlockSpec(memory_space=pltpu.VMEM)
    vmem = pltpu.VMEM
    att, gq, gk, gv = pl.pallas_call(
        kernel,
        out_shape=[jax.ShapeDtypeStruct(wide, BF16)] * 2 + [jax.ShapeDtypeStruct(own, BF16)] * 2,
        in_specs=[smem_spec] * 2 + [any_spec] * 4,
        out_specs=[any_spec] * 2 + [vmem_spec] * 2,
        scratch_shapes=[
            vmem(wide, BF16), vmem(wide, BF16), vmem(wide, BF16), vmem(wide, BF16),
            vmem((FAR + BLK_DEV * ZN, BLOCK, DH), BF16), vmem((FAR + BLK_DEV * ZN, BLOCK, DH), BF16),
            vmem((4, FAR, BLOCK, DH), BF16), vmem((2, BLK_DEV, REST, DH), BF16), vmem((4, ZN, REST, DH), BF16),
            vmem((2, ZN, 2, BLOCK, DH), BF16), vmem((2, ZN, CUT, DH), BF16),
            vmem((2, ZN, REST, DH), BF16), vmem((2, BLK_DEV, REST, DH), BF16), vmem((2, BLK_DEV, REST, DH), BF16),

            vmem((2, 2, ZN // 2, BLK_DEV, BLOCK, DH), BF16), vmem((2, ZN, BLK_DEV, BLOCK, DH), BF16),
            vmem((ENTRIES + 1, BLOCK, DH), BF16), vmem((ENTRIES + 1, BLOCK, DH), BF16),
            vmem(own, F32), vmem(own, F32),
            vmem((BLK_DEV, WIDE, DH), BF16), vmem((BLK_DEV, WIDE, DH), BF16),
            vmem((BLK_DEV, DH, WIDE), BF16), vmem((BLK_DEV, DH, WIDE), BF16),
            vmem((BLK_DEV, GROUP * BLOCK, DH), BF16), vmem((BLK_DEV, GROUP * BLOCK, DH), BF16),
            vmem((BLK_DEV, WIDE, GROUP * BLOCK), F32),
            vmem((BLK_DEV, WIDE, GROUP * BLOCK), BF16), vmem((BLK_DEV, WIDE, GROUP * BLOCK), BF16),
            vmem((WIDE, 2 * BLOCK), F32), vmem((BLK_DEV, 8, GROUP * BLOCK), F32),
            pltpu.SMEM((XN * ZN,), jnp.int32), pltpu.SMEM((XN * ZN,), jnp.int32), pltpu.SMEM((ZN,), jnp.int32), pltpu.SMEM((ENTRIES,), jnp.int32),
            pltpu.SemaphoreType.DMA((SENDS,)), pltpu.SemaphoreType.DMA((RECVS,)), pltpu.SemaphoreType.DMA((8,))],
        compiler_params=pltpu.CompilerParams(collective_id=0, has_side_effects=True, vmem_limit_bytes=56 << 20),
        name="sparse_attention",
    )(key_blocks.T, key_count, queries.reshape(wide), grad_out.reshape(wide), keys.reshape(own), values.reshape(own))
    results = [att.reshape(rows, width), gq.reshape(rows, width), gk.reshape(rows, DH), gv.reshape(rows, DH)]
    return tuple(pl.pallas_call(
        hand_on,
        out_shape=[jax.ShapeDtypeStruct(a.shape, a.dtype) for a in results],
        in_specs=[any_spec] * 4,
        out_specs=[any_spec] * 4,
        scratch_shapes=[vmem(a.shape, a.dtype) for a in results] + [pltpu.SemaphoreType.DMA((2, 4 * BLK_DEV))],
        name="hand_on",
    )(*results))


def solution(mesh):
    in_specs = (P("ctx", "head"), P("ctx", "head"), P("ctx", "head"), P("ctx", "head"), P(), P())
    out_specs = (P("ctx", "head"), P("ctx", "head"), P("ctx", "head"), P("ctx", "head"))
    return jax.shard_map(local, mesh=mesh, in_specs=in_specs, out_specs=out_specs, check_vma=False)
```
